128 devices in a mesh: ha: 16 (over z, y_hi, core), wa: 8 (over x, y_lo).
Axes of the slice: x: 4, y: 4 (y_hi: 2, y_lo: 2; y = y_hi * 2 + y_lo), z: 4, core: 2. Of those that a mesh axis runs over, the one named last changes fastest.
Arguments:
- inputs: bfloat16 [64, 512, 512], P('ha', 'wa'), may hold values from -6 to 6
- grad_out: bfloat16 [64, 512, 512], P('ha', 'wa'), may hold values from -6 to 6
- kernel_one: bfloat16 [27, 64, 64], replicated, may hold values from -0.15625 to 0.15625
- kernel_two: bfloat16 [27, 64, 64], replicated, may hold values from -0.15625 to 0.15625
Outputs:
- grad_inputs: bfloat16 [64, 512, 512], P('ha', 'wa')
- grad_kernel_one: float32 [110592], P(('ha', 'wa'))
- grad_kernel_two: float32 [110592], P(('ha', 'wa'))
The draws below stay inside these ranges and needn't reach their ends.
All inputs are finite; a program needn't handle non-finite values.
Results may differ from the reference program's by a relative error of at most 0.0049.
Values may be sent and summed in bfloat16 or wider, within the bound.
A program may use at most 64 MiB of HBM per device.

```python
import jax
import jax.numpy as jnp
from jax import lax

CH = 64
DEPTH = 8
HEIGHT = 64
WIDTH = 512


def shard_levels(rng, extent, split, smallest, top_value):
    factor_of, own = 1.0, jax.random.fold_in(rng, 6)
    for dim, blocks in split:
        heights = jnp.exp(jax.random.uniform(jax.random.fold_in(own, dim), (blocks,), jnp.float32, smallest / len(split), top_value / len(split)))
        factor_of = factor_of * jnp.repeat(heights, extent[dim] // blocks).reshape([-1 if axis == dim else 1 for axis in range(len(extent))])
    return factor_of


def normal_values(stream_key, extent, deviation, bound, split=(), dtype=jnp.bfloat16):
    entries = jax.random.normal(stream_key, extent, jnp.float32) * deviation
    if len(split) > 0:
        entries = shard_levels(stream_key, extent, split, -0.22, 0.18) * entries
    return jnp.clip(entries, min=-bound, max=bound).astype(dtype)


def setup_inputs(seed: int = 0) -> dict:
    key_of = jax.random.split(jax.random.key(seed), 5)
    return {
        "inputs": normal_values(key_of[0], (HEIGHT, WIDTH, DEPTH * CH), 1.0, 6.0, ((0, 16), (1, 8))),
        "grad_out": normal_values(key_of[1], (HEIGHT, WIDTH, DEPTH * CH), 1.0, 6.0, ((0, 16), (1, 8))),
        "kernel_one": normal_values(key_of[2], (27, CH, CH), (27 * CH) ** -0.5, 0.15625),
        "kernel_two": normal_values(key_of[3], (27, CH, CH), (27 * CH) ** -0.5, 0.15625),
    }


root_half = 0.7071067811865476
inv_root_two_pi = 0.3989422804014327

def gelu_value(values):
    return 0.5 * values * (1.0 + jax.scipy.special.erf(values * root_half))

def gelu_slope(values):
    return 0.5 * (1.0 + jax.scipy.special.erf(values * root_half)) + values * inv_root_two_pi * jnp.exp(-0.5 * values * values)

def flip_kernel(kernel):
    return jnp.swapaxes(kernel[::-1], 1, 2)

def correlate(volume, kernel):
    left = volume.astype(jnp.float32)[None]
    right = kernel.astype(jnp.float32).reshape(3, 3, 3, kernel.shape[1], kernel.shape[2])
    result = lax.conv_general_dilated(left, right, (1, 1, 1), ((1, 1), (1, 1), (1, 1)), dimension_numbers=('NDHWC', 'DHWIO', 'NDHWC'), precision=lax.Precision.HIGHEST)
    return result[0]

def kernel_grad(source, cotangent):
    rows_here, cols_here, depth_cells, chans = cotangent.shape
    padded = jnp.pad(source, ((1, 1), (1, 1), (1, 1), (0, 0)))
    flat_cot = cotangent.astype(jnp.float32).reshape(-1, chans)
    pieces = []
    for position in range(27):
        rise_shift, side_shift, deep_shift = (position // 9, position // 3 % 3, position % 3)
        window = padded[rise_shift:rise_shift + rows_here, side_shift:side_shift + cols_here, deep_shift:deep_shift + depth_cells]
        window = window.astype(jnp.float32).reshape(-1, chans)
        pieces.append(jnp.dot(window.T, flat_cot, precision=lax.Precision.HIGHEST))
    return jnp.stack(pieces)

def reference(inputs, grad_out, kernel_one, kernel_two):
    volume = inputs.reshape(HEIGHT, WIDTH, DEPTH, CH)
    cotangent = grad_out.reshape(HEIGHT, WIDTH, DEPTH, CH)
    pre_active = correlate(volume, kernel_one)
    active = gelu_value(pre_active).astype(jnp.bfloat16)
    grad_active = correlate(cotangent, flip_kernel(kernel_two))
    grad_pre = (grad_active * gelu_slope(pre_active)).astype(jnp.bfloat16)
    grad_inputs = correlate(grad_pre, flip_kernel(kernel_one)).astype(jnp.bfloat16).reshape(HEIGHT, WIDTH, DEPTH * CH)
    grad_kernel_one = kernel_grad(volume, grad_pre).reshape(-1)
    grad_kernel_two = kernel_grad(active, cotangent).reshape(-1)
    return (grad_inputs, grad_kernel_one, grad_kernel_two)
```

```python
import functools

import jax
import jax.numpy as jnp
from jax import lax
from jax.experimental import pallas as pl
from jax.experimental.pallas import tpu as pltpu
from jax.sharding import PartitionSpec as P

CH = 64
DEPTH = 8
TAPS = 27
LANES = DEPTH * CH
PADDED = LANES + 2 * CH
QUAD = 4 * CH
WINDOW = 6 * CH
KTOTAL = 9 * WINDOW
MESH = pl.DeviceIdType.MESH
F32 = jnp.float32
BF16 = jnp.bfloat16

root_half = 0.7071067811865476
inv_root_two_pi = 0.3989422804014327


def round_up(value, multiple):
    return -(-value // multiple) * multiple


def kernel(
    sizes,
    x_hbm,
    g_hbm,
    k1_hbm,
    k2_hbm,
    gi_hbm,
    fin_ref,
    xl,
    gl,
    kraw,
    kd,
    w1,
    w2,
    w3,
    esend,
    erecv,
    rowbuf,
    shifted,
    gpl,
    active,
    gout,
    packed,
    piece,
    got,
    total,
    window,
    wgot,
    out_buf,
    local_sem,
    halo_send,
    halo_recv,
    first_send,
    first_recv,
    second_send,
    second_recv,
):
    n_ha, n_wa, rows, cols = sizes
    ha = lax.axis_index("ha")
    wa = lax.axis_index("wa")
    cells = rows * cols
    rows_first = (TAPS * CH) // n_ha
    first_pad = piece.shape[1]
    win_pad = window.shape[1]

    def ha_at(step):
        return lax.rem(ha + (step + n_ha), n_ha)

    def wa_at(step):
        return lax.rem(wa + (step + n_wa), n_wa)

    barrier = pltpu.get_barrier_semaphore()
    peers = [(ha_at(d), wa) for d in range(1, n_ha)]
    peers += [(ha, wa_at(d)) for d in range(1, n_wa)]
    peers += [(ha_at(a), wa_at(b)) for a in (-1, 1) for b in (-1, 1)]
    for peer in peers:
        pl.semaphore_signal(barrier, inc=1, device_id=peer, device_id_type=MESH)

    loads = [
        pltpu.make_async_copy(k1_hbm, kraw.at[0], local_sem.at[0]),
        pltpu.make_async_copy(k2_hbm, kraw.at[1], local_sem.at[1]),
        pltpu.make_async_copy(x_hbm, xl, local_sem.at[2]),
        pltpu.make_async_copy(g_hbm, gl, local_sem.at[3]),
    ]
    for load in loads:
        load.start()

    def edges(field_refs, side):
        start, pick = (0, 0) if side == 0 else (cols - 16, 15)
        ids = lax.broadcasted_iota(jnp.int32, (16, LANES), 0)
        value = jnp.zeros((16, LANES), F32)
        for f, ref in enumerate(field_refs):
            for h in range(rows):
                block = ref[h, start : start + 16, :].astype(F32)
                cell = jnp.broadcast_to(block[pick : pick + 1], (16, LANES))
                value = jnp.where(ids == f * 8 + h, cell, value)
        return value.astype(BF16)

    def exchange(phase, field_refs):
        copies = []
        for f, ref in enumerate(field_refs):
            slot = phase * 2 + f
            for side, row, step in ((0, rows - 1, 1), (1, 0, -1)):
                copies.append(
                    pltpu.make_async_remote_copy(
                        src_ref=ref.at[row],
                        dst_ref=rowbuf.at[slot, side],
                        send_sem=halo_send.at[phase, f * 2 + side],
                        recv_sem=halo_recv.at[phase, f * 2 + side],
                        device_id=(ha_at(step), wa),
                        device_id_type=MESH,
                    )
                )
        for side, wa_step in ((0, -1), (1, 1)):
            for dh in (-1, 0, 1):
                slot = (1 - side) * 3 + 1 - dh
                copies.append(
                    pltpu.make_async_remote_copy(
                        src_ref=esend.at[phase, side],
                        dst_ref=erecv.at[phase, slot],
                        send_sem=halo_send.at[phase, 4 + slot],
                        recv_sem=halo_recv.at[phase, 4 + slot],
                        device_id=(ha_at(dh), wa_at(wa_step)),
                        device_id_type=MESH,
                    )
                )
        for copy in copies:
            copy.start()
        return copies

    def widen(value):
        zeros = jnp.zeros((value.shape[0], PADDED - LANES), F32)
        return pltpu.roll(jnp.concatenate([value, zeros], axis=1), CH, 1)

    low_ok = ha > 0
    high_ok = ha < n_ha - 1
    left_ok = wa > 0
    right_ok = wa < n_wa - 1
    cell_ids = lax.broadcasted_iota(jnp.int32, (cols, PADDED), 0)

    def prepare(phase, f, ref, dst):
        slot = phase * 2 + f
        oks = (low_ok, None, high_ok)
        halo_cells = []
        for side, ok in ((0, left_ok), (1, right_ok)):
            group = []
            for r in range(3):
                value = widen(erecv[phase, side * 3 + r].astype(F32))
                good = ok if oks[r] is None else jnp.logical_and(ok, oks[r])
                group.append(jnp.where(good, value, 0.0))
            halo_cells.append(group)
        for e in range(rows + 2):
            if e == 0:
                value = jnp.where(low_ok, rowbuf[slot, 0].astype(F32), 0.0)
                r, h = 0, rows - 1
            elif e == rows + 1:
                value = jnp.where(high_ok, rowbuf[slot, 1].astype(F32), 0.0)
                r, h = 2, 0
            else:
                value = ref[e - 1].astype(F32)
                r, h = 1, e - 1
            value = widen(value)
            left = halo_cells[0][r][f * 8 + h : f * 8 + h + 1]
            right = halo_cells[1][r][f * 8 + h : f * 8 + h + 1]
            before = jnp.where(
                cell_ids == 0,
                jnp.broadcast_to(left, (cols, PADDED)),
                pltpu.roll(value, 1, 0),
            )
            after = jnp.where(
                cell_ids == cols - 1,
                jnp.broadcast_to(right, (cols, PADDED)),
                pltpu.roll(value, cols - 1, 0),
            )
            shifted[dst, 0, e] = before.astype(BF16)
            shifted[dst, 1, e] = value.astype(BF16)
            shifted[dst, 2, e] = after.astype(BF16)

    lane_low = lax.broadcasted_iota(jnp.int32, (CH, 2 * CH), 1) < CH
    zero_block = jnp.zeros((CH, 2 * CH), BF16)

    def double(which):
        @pl.loop(0, TAPS)
        def _(t):
            block = kraw[which, t].astype(F32)
            kd[which, t] = jnp.concatenate([block, block], axis=1).astype(BF16)

    def build_rows(which, dst):
        @pl.loop(0, 9)
        def _(ab):
            for di in range(6):
                for m in range(2):
                    parts = []
                    for do in (2 * m, 2 * m + 1):
                        c = di - do
                        parts.append(kd[which, ab * 3 + c] if 0 <= c <= 2 else zero_block)
                    start = pl.multiple_of(ab * WINDOW + di * CH, CH)
                    dst[pl.ds(start, CH), m * 128 : m * 128 + 128] = jnp.where(
                        lane_low, parts[0], parts[1]
                    )

    def build_turned(which, dst):
        @pl.loop(0, 9)
        def _(ab):
            for do in range(4):
                for m in range(3):
                    parts = []
                    for di in (2 * m, 2 * m + 1):
                        c = di - do
                        parts.append(
                            kd[which, TAPS - 1 - (ab * 3 + c)] if 0 <= c <= 2 else zero_block
                        )
                    start = pl.multiple_of(ab * WINDOW + m * 128, 128)
                    dst[do * CH : (do + 1) * CH, pl.ds(start, 128)] = jnp.where(
                        lane_low, parts[0], parts[1]
                    )

    loads[2].wait()
    loads[3].wait()
    for side in range(2):
        esend[0, side] = edges((xl, gl), side)
    pl.semaphore_wait(barrier, len(peers))
    halos = exchange(0, (xl, gl))

    loads[0].wait()
    loads[1].wait()
    double(0)
    double(1)
    build_rows(0, w1)
    build_turned(1, w2)
    build_turned(0, w3)

    for copy in halos:
        copy.wait()
    prepare(0, 0, xl, 0)
    prepare(0, 1, gl, 1)

    def stacked(src, q):
        return jnp.concatenate(
            [
                shifted[src, b, a : a + rows, :, q * QUAD : q * QUAD + WINDOW].reshape(
                    cells, WINDOW
                )
                for a in range(3)
                for b in range(3)
            ],
            axis=1,
        )

    def conv(src, q, weights, turned):
        dims = (((1,), (1,)), ((), ())) if turned else (((1,), (0,)), ((), ()))
        return lax.dot_general(stacked(src, q), weights[...], dims, preferred_element_type=F32)

    for q in range(2):
        pre = conv(0, q, w1, False)
        grad_active = conv(1, q, w2, True)
        phi = 0.5 * (1.0 + lax.erf(pre * root_half))
        active[q] = (pre * phi).astype(BF16)
        slope = phi + pre * inv_root_two_pi * jnp.exp(-0.5 * pre * pre)
        grad_pre = (grad_active * slope).astype(BF16)
        gpl[:, :, q * QUAD : (q + 1) * QUAD] = grad_pre.reshape(rows, cols, QUAD)

    for side in range(2):
        esend[1, side] = edges((gpl,), side)
    halos = exchange(1, (gpl,))

    half = lax.broadcasted_iota(jnp.int32, (CH, 128), 1) < CH
    flip_dims = (((0,), (0,)), ((), ()))

    def diagonals(value):
        blocks = [value[d * CH : (d + 1) * CH] for d in range(4)]
        even = [blocks[0][:, i * 128 : i * 128 + 128] + blocks[2][:, (i + 1) * 128 : (i + 1) * 128 + 128] for i in range(2)]
        odd = [blocks[1][:, i * 128 : i * 128 + 128] + blocks[3][:, (i + 1) * 128 : (i + 1) * 128 + 128] for i in range(2)]
        return even, odd

    @pl.loop(0, 9)
    def _(ab):
        a = ab // 3
        b = ab - a * 3
        one = jnp.zeros((QUAD, WINDOW), F32)
        two = jnp.zeros((QUAD, WINDOW), F32)
        for q in range(2):
            lanes = slice(q * QUAD, q * QUAD + WINDOW)
            xw = shifted[0, b, pl.ds(a, rows), :, lanes].reshape(cells, WINDOW)
            gw = shifted[1, 2 - b, pl.ds(2 - a, rows), :, lanes].reshape(cells, WINDOW)
            gp = gpl[:, :, q * QUAD : (q + 1) * QUAD].reshape(cells, QUAD)
            one += lax.dot_general(gp, xw, flip_dims, preferred_element_type=F32)
            two += lax.dot_general(active[q], gw, flip_dims, preferred_element_type=F32)
        even, odd = diagonals(one)
        turn = [pltpu.roll(v, CH, 1) for v in odd]
        first = even[0] + jnp.where(half, turn[0], turn[1])
        second = even[1] + turn[1]
        kernel_one = jnp.concatenate([first.T, second.T[:CH]], axis=0)
        even, odd = diagonals(two)
        turn = [pltpu.roll(v, CH, 1) for v in even]
        third = odd[0] + turn[0]
        mid = even[0] + jnp.where(half, pltpu.roll(odd[0], CH, 1), pltpu.roll(odd[1], CH, 1))
        last = odd[1] + turn[1]
        kernel_two = jnp.concatenate([last, mid, third], axis=0)
        start = pl.multiple_of(ab * 3 * CH, CH)
        packed[pl.ds(start, 3 * CH), :] = jnp.concatenate(
            [kernel_one, kernel_two[:, CH:]], axis=1
        )

    for j in range(n_ha):
        piece[j, 0:rows_first, :] = packed[j * rows_first : (j + 1) * rows_first, :].astype(BF16)
    firsts = []
    for d in range(1, n_ha):
        to = ha_at(d)
        firsts.append(
            pltpu.make_async_remote_copy(
                src_ref=piece.at[to],
                dst_ref=got.at[d],
                send_sem=first_send.at[d],
                recv_sem=first_recv.at[d],
                device_id=(to, wa),
                device_id_type=MESH,
            )
        )
    for copy in firsts:
        copy.start()

    for copy in halos:
        copy.wait()
    prepare(1, 0, gpl, 2)
    for q in range(2):
        value = conv(2, q, w3, True).astype(BF16)
        gout[:, :, q * QUAD : (q + 1) * QUAD] = value.reshape(rows, cols, QUAD)
    store = pltpu.make_async_copy(gout, gi_hbm, local_sem.at[4])
    store.start()

    for copy in firsts:
        copy.wait()
    value = piece[ha].astype(F32)
    for d in range(1, n_ha):
        value += got[d].astype(F32)
    total[...] = value
    starts = [(k * rows_first) // n_wa for k in range(n_wa)]
    for k in range(n_wa):
        count = min(win_pad, first_pad - starts[k])
        window[k, 0:count, :] = total[starts[k] : starts[k] + count, :]
    seconds = []
    for d in range(1, n_wa):
        to = wa_at(d)
        seconds.append(
            pltpu.make_async_remote_copy(
                src_ref=window.at[to],
                dst_ref=wgot.at[d],
                send_sem=second_send.at[d],
                recv_sem=second_recv.at[d],
                device_id=(ha, to),
                device_id_type=MESH,
            )
        )
    for copy in seconds:
        copy.start()
    for copy in seconds:
        copy.wait()
    value = window[wa]
    for d in range(1, n_wa):
        value += wgot[d]
    fin_ref[...] = value
    store.wait()


def shards(sizes, inputs, grad_out, kernel_one, kernel_two):
    n_ha, n_wa, rows, cols = sizes
    rows_first = (TAPS * CH) // n_ha
    first_pad = round_up(rows_first, 16)
    exact = (TAPS * CH * CH) // (n_ha * n_wa)
    win = -(-exact // CH) + (1 if exact % CH else 0)
    win_pad = round_up(win, 8)
    any_spec = pl.BlockSpec(memory_space=pl.ANY)
    dma = pltpu.SemaphoreType.DMA
    grad_inputs, fin = pl.pallas_call(
        functools.partial(kernel, sizes),
        out_shape=(
            jax.ShapeDtypeStruct((rows, cols, LANES), BF16),
            jax.ShapeDtypeStruct((win_pad, 2 * CH), F32),
        ),
        in_specs=[any_spec] * 4,
        out_specs=(any_spec, pl.BlockSpec(memory_space=pltpu.VMEM)),
        scratch_shapes=[
            pltpu.VMEM((rows, cols, LANES), BF16),
            pltpu.VMEM((rows, cols, LANES), BF16),
            pltpu.VMEM((2, TAPS, CH, CH), BF16),
            pltpu.VMEM((2, TAPS, CH, 2 * CH), BF16),
            pltpu.VMEM((KTOTAL, QUAD), BF16),
            pltpu.VMEM((QUAD, KTOTAL), BF16),
            pltpu.VMEM((QUAD, KTOTAL), BF16),
            pltpu.VMEM((2, 2, 16, LANES), BF16),
            pltpu.VMEM((2, 6, 16, LANES), BF16),
            pltpu.VMEM((3, 2, cols, LANES), BF16),
            pltpu.VMEM((3, 3, rows + 2, cols, PADDED), BF16),
            pltpu.VMEM((rows, cols, LANES), BF16),
            pltpu.VMEM((2, rows * cols, QUAD), BF16),
            pltpu.VMEM((rows, cols, LANES), BF16),
            pltpu.VMEM((TAPS * CH, 2 * CH), F32),
            pltpu.VMEM((n_ha, first_pad, 2 * CH), BF16),
            pltpu.VMEM((n_ha, first_pad, 2 * CH), BF16),
            pltpu.VMEM((first_pad, 2 * CH), F32),
            pltpu.VMEM((n_wa, win_pad, 2 * CH), F32),
            pltpu.VMEM((n_wa, win_pad, 2 * CH), F32),
            pltpu.VMEM((8, 128), F32),
            dma((5,)),
            dma((2, 10)),
            dma((2, 10)),
            dma((n_ha,)),
            dma((n_ha,)),
            dma((n_wa,)),
            dma((n_wa,)),
        ],
        compiler_params=pltpu.CompilerParams(
            collective_id=0, has_side_effects=True, vmem_limit_bytes=60 * 1024 * 1024
        ),
    )(inputs, grad_out, kernel_one, kernel_two)
    wa = lax.axis_index("wa")
    begin = (wa * (exact * n_wa)) // n_wa - ((wa * rows_first) // n_wa) * CH
    begin = wa * exact - ((wa * rows_first) // n_wa) * CH

    def cut(lanes):
        flat = fin[:win, lanes].reshape(-1)
        return lax.dynamic_slice(flat, (begin,), (exact,))

    return grad_inputs, cut(slice(0, CH)), cut(slice(CH, 2 * CH))


def solution(mesh):
    n_ha, n_wa = mesh.shape["ha"], mesh.shape["wa"]

    def step(inputs, grad_out, kernel_one, kernel_two):
        rows, cols, _ = inputs.shape
        return shards((n_ha, n_wa, rows, cols), inputs, grad_out, kernel_one, kernel_two)

    return jax.shard_map(
        step,
        mesh=mesh,
        in_specs=(P("ha", "wa", None), P("ha", "wa", None), P(), P()),
        out_specs=(P("ha", "wa", None), P(("ha", "wa")), P(("ha", "wa"))),
        check_vma=False,
    )
```

```python
import functools

import jax
import jax.numpy as jnp
from jax import lax
from jax.experimental import pallas as pl
from jax.experimental.pallas import tpu as pltpu
from jax.sharding import PartitionSpec as P

CH = 64
DEPTH = 8
TAPS = 27
LANES = DEPTH * CH
PADDED = LANES + 2 * CH
PAIR = 2 * CH
PATCH = 4 * CH
KTOTAL = 3 * 16 * CH
MESH = pl.DeviceIdType.MESH
F32 = jnp.float32
BF16 = jnp.bfloat16

root_half = 0.7071067811865476
inv_root_two_pi = 0.3989422804014327


def round_up(value, multiple):
    return -(-value // multiple) * multiple


def kernel(
    sizes,
    x_hbm,
    g_hbm,
    k1_hbm,
    k2_hbm,
    gi_ref,
    fin_ref,
    xl,
    gl,
    kraw,
    kd,
    w1,
    w2,
    w3,
    esend,
    erecv,
    rowbuf,
    shifted,
    gpl,
    turned,
    sums,
    piece,
    got,
    total,
    window,
    wgot,
    local_sem,
    halo_send,
    halo_recv,
    first_send,
    first_recv,
    second_send,
    second_recv,
):
    n_ha, n_wa, rows, cols = sizes
    ha = lax.axis_index("ha")
    wa = lax.axis_index("wa")
    pairs = rows // 2
    rows_first = (TAPS * CH) // (2 * n_ha)
    exact = (TAPS * CH * CH) // (n_ha * n_wa)

    def wrap(value, size):
        value = jnp.where(value >= size, value - size, value)
        return jnp.where(value < 0, value + size, value)

    def ha_at(step):
        return wrap(ha + step, n_ha)

    def wa_at(step):
        return wrap(wa + step, n_wa)

    barrier = pltpu.get_barrier_semaphore()
    peers = [(ha_at(d), wa) for d in range(1, n_ha)]
    peers += [(ha, wa_at(d)) for d in range(1, n_wa)]
    peers += [(ha_at(a), wa_at(b)) for a in (-1, 1) for b in (-1, 1)]
    loads = [
        pltpu.make_async_copy(x_hbm, xl, local_sem.at[2]),
        pltpu.make_async_copy(g_hbm, gl, local_sem.at[3]),
        pltpu.make_async_copy(k1_hbm, kraw.at[0], local_sem.at[0]),
        pltpu.make_async_copy(k2_hbm, kraw.at[1], local_sem.at[1]),
    ]
    for load in loads:
        load.start()
    for peer in peers:
        pl.semaphore_signal(barrier, inc=1, device_id=peer, device_id_type=MESH)

    def edges(field_refs, side):
        start, pick = (0, 0) if side == 0 else (cols - 16, 15)
        ids = lax.broadcasted_iota(jnp.int32, (16, LANES), 0)
        value = jnp.zeros((16, LANES), F32)
        for f, ref in enumerate(field_refs):
            for h in range(rows):
                block = ref[h, start : start + 16, :].astype(F32)
                cell = jnp.broadcast_to(block[pick : pick + 1], (16, LANES))
                value = jnp.where(ids == f * 8 + h, cell, value)
        return value.astype(BF16)

    def exchange(phase, field_refs):
        copies = []
        for f, ref in enumerate(field_refs):
            slot = phase * 2 + f
            for side, row, step in ((0, rows - 1, 1), (1, 0, -1)):
                copies.append(
                    pltpu.make_async_remote_copy(
                        src_ref=ref.at[row],
                        dst_ref=rowbuf.at[slot, side],
                        send_sem=halo_send.at[phase, f * 2 + side],
                        recv_sem=halo_recv.at[phase, f * 2 + side],
                        device_id=(ha_at(step), wa),
                        device_id_type=MESH,
                    )
                )
        for side, wa_step in ((0, -1), (1, 1)):
            for dh in (-1, 0, 1):
                slot = (1 - side) * 3 + 1 - dh
                copies.append(
                    pltpu.make_async_remote_copy(
                        src_ref=esend.at[phase, side],
                        dst_ref=erecv.at[phase, slot],
                        send_sem=halo_send.at[phase, 4 + slot],
                        recv_sem=halo_recv.at[phase, 4 + slot],
                        device_id=(ha_at(dh), wa_at(wa_step)),
                        device_id_type=MESH,
                    )
                )
        for copy in copies:
            copy.start()
        return copies

    def widen(value):
        zeros = jnp.zeros((value.shape[0], PADDED - LANES), F32)
        return pltpu.roll(jnp.concatenate([value, zeros], axis=1), CH, 1)

    low_ok = ha > 0
    high_ok = ha < n_ha - 1
    left_ok = wa > 0
    right_ok = wa < n_wa - 1
    cell_ids = lax.broadcasted_iota(jnp.int32, (cols, PADDED), 0)
    tile_ids = lax.broadcasted_iota(jnp.int32, (16, PADDED), 0)

    def own_rows(ref, dst):
        for h in range(rows):
            value = widen(ref[h].astype(F32))
            shifted[dst, 0, h + 1] = pltpu.roll(value, 1, 0).astype(BF16)
            shifted[dst, 1, h + 1] = value.astype(BF16)
            shifted[dst, 2, h + 1] = pltpu.roll(value, cols - 1, 0).astype(BF16)

    def finish_rows(phase, f, dst):
        slot = phase * 2 + f
        oks = (low_ok, None, high_ok)
        halo_cells = []
        for side, ok in ((0, left_ok), (1, right_ok)):
            group = []
            for r in range(3):
                value = widen(erecv[phase, side * 3 + r].astype(F32))
                good = ok if oks[r] is None else jnp.logical_and(ok, oks[r])
                group.append(jnp.where(good, value, 0.0))
            halo_cells.append(group)
        for h in range(rows):
            left = halo_cells[0][1][f * 8 + h : f * 8 + h + 1]
            right = halo_cells[1][1][f * 8 + h : f * 8 + h + 1]
            tile = shifted[dst, 0, h + 1, 0:16, :].astype(F32)
            tile = jnp.where(tile_ids == 0, jnp.broadcast_to(left, (16, PADDED)), tile)
            shifted[dst, 0, h + 1, 0:16, :] = tile.astype(BF16)
            tile = shifted[dst, 2, h + 1, cols - 16 : cols, :].astype(F32)
            tile = jnp.where(tile_ids == 15, jnp.broadcast_to(right, (16, PADDED)), tile)
            shifted[dst, 2, h + 1, cols - 16 : cols, :] = tile.astype(BF16)
        for e, side, ok, r, h in ((0, 0, low_ok, 0, rows - 1), (rows + 1, 1, high_ok, 2, 0)):
            value = widen(jnp.where(ok, rowbuf[slot, side].astype(F32), 0.0))
            left = halo_cells[0][r][f * 8 + h : f * 8 + h + 1]
            right = halo_cells[1][r][f * 8 + h : f * 8 + h + 1]
            before = jnp.where(
                cell_ids == 0,
                jnp.broadcast_to(left, (cols, PADDED)),
                pltpu.roll(value, 1, 0),
            )
            after = jnp.where(
                cell_ids == cols - 1,
                jnp.broadcast_to(right, (cols, PADDED)),
                pltpu.roll(value, cols - 1, 0),
            )
            shifted[dst, 0, e] = before.astype(BF16)
            shifted[dst, 1, e] = value.astype(BF16)
            shifted[dst, 2, e] = after.astype(BF16)

    lane_low = lax.broadcasted_iota(jnp.int32, (CH, PAIR), 1) < CH
    zero_block = jnp.zeros((CH, PAIR), BF16)

    def double():
        @pl.loop(0, 9)
        def _(ab):
            for c in range(3):
                for which in range(2):
                    block = kraw[which, ab * 3 + c]
                    kd[which, ab * 3 + c] = jnp.concatenate([block, block], axis=1)

    def tap_block(which, index, c):
        return kd[which, index(c)] if 0 <= c <= 2 else zero_block

    def build_rows(which, dst):
        @pl.loop(0, 3)
        def _(b):
            base = b * 16 * CH
            for di in range(4):
                for a in range(4):
                    if a < 3:
                        index = lambda c: 9 * a + 3 * b + c
                        tile = jnp.where(
                            lane_low,
                            tap_block(which, index, di),
                            tap_block(which, index, di - 1),
                        )
                    else:
                        tile = zero_block
                    here = pl.multiple_of(base + (a * 4 + di) * CH, CH)
                    dst[pl.ds(here, CH), 0:PAIR] = tile
                    here = pl.multiple_of(base + ((a + 1) % 4 * 4 + di) * CH, CH)
                    dst[pl.ds(here, CH), PAIR : 2 * PAIR] = tile

    def build_turned(which, dst):
        @pl.loop(0, 3)
        def _(b):
            base = b * 16 * CH
            for dd in range(2):
                for m in range(2):
                    for a in range(4):
                        if a < 3:
                            index = lambda c: TAPS - 1 - (9 * a + 3 * b + c)
                            tile = jnp.where(
                                lane_low,
                                tap_block(which, index, 2 * m - dd),
                                tap_block(which, index, 2 * m + 1 - dd),
                            )
                        else:
                            tile = zero_block
                        here = pl.multiple_of(base + (a * 4 + 2 * m) * CH, 128)
                        dst[dd * CH : (dd + 1) * CH, pl.ds(here, PAIR)] = tile
                        here = pl.multiple_of(base + ((a + 1) % 4 * 4 + 2 * m) * CH, 128)
                        dst[PAIR + dd * CH : PAIR + (dd + 1) * CH, pl.ds(here, PAIR)] = tile

    loads[0].wait()
    loads[1].wait()
    for side in range(2):
        esend[0, side] = edges((xl, gl), side)
    pl.semaphore_wait(barrier, len(peers))
    halos = exchange(0, (xl, gl))

    loads[2].wait()
    loads[3].wait()
    double()
    build_rows(0, w1)
    build_turned(1, w2)
    build_turned(0, w3)
    own_rows(xl, 0)
    own_rows(gl, 1)

    for copy in halos:
        copy.wait()
    finish_rows(0, 0, 0)
    finish_rows(0, 1, 1)

    def patches(src, b, i, hp):
        return jnp.concatenate(
            [
                shifted[src, b, 2 * hp + i, :, dp * PAIR : dp * PAIR + PATCH]
                for dp in range(DEPTH // 2)
            ],
            axis=0,
        )

    def conv(src, hp, weights, flipped):
        left = jnp.concatenate(
            [patches(src, b, i, hp) for b in range(3) for i in range(4)], axis=1
        )
        dims = (((1,), (1,)), ((), ())) if flipped else (((1,), (0,)), ((), ()))
        return lax.dot_general(left, weights[...], dims, preferred_element_type=F32)

    def spread(dst, hp, value):
        for hh in range(2):
            for dp in range(DEPTH // 2):
                dst[2 * hp + hh, :, dp * PAIR : (dp + 1) * PAIR] = value[
                    dp * cols : (dp + 1) * cols, hh * PAIR : (hh + 1) * PAIR
                ]

    block = cols * (DEPTH // 2)
    for hp in range(pairs):
        pre = conv(0, hp, w1, False)
        grad_active = conv(1, hp, w2, True)
        phi = 0.5 * (1.0 + lax.erf(pre * root_half))
        active = (pre * phi).astype(BF16)
        slope = phi + pre * inv_root_two_pi * jnp.exp(-0.5 * pre * pre)
        grad_pre = (grad_active * slope).astype(BF16)
        spread(gpl, hp, grad_pre)
        turned[0, :, hp * block : (hp + 1) * block] = grad_pre.T
        turned[1, :, hp * block : (hp + 1) * block] = active.T

    for side in range(2):
        esend[1, side] = edges((gpl,), side)
    halos = exchange(1, (gpl,))

    half = lax.broadcasted_iota(jnp.int32, (CH, PAIR), 1) < CH

    def gradients(src, b):
        blocks = []
        for i in range(4):
            right = jnp.concatenate([patches(src, b, i, hp) for hp in range(pairs)], axis=0)
            blocks.append(
                lax.dot_general(
                    turned[src],
                    right,
                    (((1,), (0,)), ((), ())),
                    preferred_element_type=F32,
                )
            )
        for a in range(3):
            low, high = blocks[a], blocks[a + 1]
            even = low[0:CH] + high[PAIR : PAIR + CH]
            odd = low[CH:PAIR] + high[PAIR + CH : 2 * PAIR]
            yield a, even[:, :PAIR], even[:, PAIR:], odd[:, :PAIR], odd[:, PAIR:]

    def send_pieces(which):
        for j in range(n_ha):
            first = sums[which, pl.ds(2 * j * rows_first, rows_first, stride=2), :]
            second = sums[which, pl.ds(2 * j * rows_first + 1, rows_first, stride=2), :]
            value = jnp.where(
                lax.broadcasted_iota(jnp.int32, (rows_first, PAIR), 1) < CH,
                first,
                pltpu.roll(second, CH, 1),
            )
            piece[which, j, 0:rows_first, :] = value.astype(BF16)
        copies = []
        for d in range(1, n_ha):
            to = ha_at(d)
            copies.append(
                pltpu.make_async_remote_copy(
                    src_ref=piece.at[which, to],
                    dst_ref=got.at[which, d],
                    send_sem=first_send.at[which, d],
                    recv_sem=first_recv.at[which, d],
                    device_id=(to, wa),
                    device_id_type=MESH,
                )
            )
        for copy in copies:
            copy.start()
        return copies

    for b in range(3):
        for a, even0, even1, odd0, odd1 in gradients(1, b):
            turn = pltpu.roll(odd1, CH, 1)
            values = (even0 + pltpu.roll(odd0, CH, 1), odd1 + pltpu.roll(even0, CH, 1), even1 + turn)
            for c in range(3):
                start = (TAPS - 1 - (9 * a + 3 * b + c)) * CH
                sums[1, start : start + CH, :] = values[c]
    firsts = [None, send_pieces(1)]
    for b in range(3):
        for a, even0, even1, odd0, odd1 in gradients(0, b):
            turn = pltpu.roll(odd1, CH, 1)
            both = even0 + jnp.where(half, pltpu.roll(odd0, CH, 1), turn)
            start = (9 * a + 3 * b) * CH
            sums[0, start : start + 2 * CH, 0:CH] = both.T
            sums[0, start + 2 * CH : start + 3 * CH, 0:CH] = (even1 + turn).T[0:CH]
    firsts[0] = send_pieces(0)

    own_rows(gpl, 2)
    for copy in halos:
        copy.wait()
    finish_rows(1, 0, 2)
    for hp in range(pairs):
        spread(gi_ref, hp, conv(2, hp, w3, True).astype(BF16))

    starts = [(k * rows_first) // n_wa for k in range(n_wa)]
    span = window.shape[2]
    for which in (1, 0):
        for copy in firsts[which]:
            copy.wait()
        value = piece[which, ha].astype(F32)
        for d in range(1, n_ha):
            value += got[which, d].astype(F32)
        total[...] = value
        for k in range(n_wa):
            window[k, which] = total[starts[k] : starts[k] + span, :]
    seconds = []
    for d in range(1, n_wa):
        to = wa_at(d)
        seconds.append(
            pltpu.make_async_remote_copy(
                src_ref=window.at[to],
                dst_ref=wgot.at[d],
                send_sem=second_send.at[d],
                recv_sem=second_recv.at[d],
                device_id=(ha, to),
                device_id_type=MESH,
            )
        )
    for copy in seconds:
        copy.start()
    for copy in seconds:
        copy.wait()
    value = window[wa]
    for d in range(1, n_wa):
        value += wgot[d]
    fin_ref[...] = value


def finish(sizes, gi_ref, fin_ref, gi_hbm, one_ref, two_ref, sem):
    n_ha, n_wa, rows, cols = sizes
    wa = lax.axis_index("wa")
    exact = (TAPS * CH * CH) // (n_ha * n_wa)
    store = pltpu.make_async_copy(gi_ref, gi_hbm, sem)
    store.start()
    offset = lax.rem(wa * exact, 128)
    count = -(-exact // 128)
    lanes = lax.broadcasted_iota(jnp.int32, (count, 128), 1)
    for which, out in ((0, one_ref), (1, two_ref)):
        value = pltpu.roll(fin_ref[which], 128 - offset, 1)
        value = jnp.where(lanes < 128 - offset, value[0:count], value[1 : count + 1])
        for r in range(count):
            width = min(128, exact - r * 128)
            out[pl.ds(r * 128, width)] = value[r, 0:width]
    store.wait()


def shards(sizes, inputs, grad_out, kernel_one, kernel_two):
    n_ha, n_wa, rows, cols = sizes
    rows_first = (TAPS * CH) // (2 * n_ha)
    exact = (TAPS * CH * CH) // (n_ha * n_wa)
    out_rows = -(-exact // 128)
    span = round_up(out_rows + 1, 8)
    first_pad = round_up(max(rows_first, (n_wa - 1) * rows_first // n_wa + span), 16)
    any_spec = pl.BlockSpec(memory_space=pl.ANY)
    vmem_spec = pl.BlockSpec(memory_space=pltpu.VMEM)
    dma = pltpu.SemaphoreType.DMA
    grad_inputs, fin = pl.pallas_call(
        functools.partial(kernel, sizes),
        out_shape=(
            pltpu.VMEM((rows, cols, LANES), BF16),
            pltpu.VMEM((2, span, 128), F32),
        ),
        in_specs=[pl.BlockSpec(memory_space=pltpu.HBM)] * 4,
        out_specs=(vmem_spec, vmem_spec),
        scratch_shapes=[
            pltpu.VMEM((rows, cols, LANES), BF16),
            pltpu.VMEM((rows, cols, LANES), BF16),
            pltpu.VMEM((2, TAPS, CH, CH), BF16),
            pltpu.VMEM((2, TAPS, CH, PAIR), BF16),
            pltpu.VMEM((KTOTAL, PATCH), BF16),
            pltpu.VMEM((PATCH, KTOTAL), BF16),
            pltpu.VMEM((PATCH, KTOTAL), BF16),
            pltpu.VMEM((2, 2, 16, LANES), BF16),
            pltpu.VMEM((2, 6, 16, LANES), BF16),
            pltpu.VMEM((3, 2, cols, LANES), BF16),
            pltpu.VMEM((3, 3, rows + 2, cols, PADDED), BF16),
            pltpu.VMEM((rows, cols, LANES), BF16),
            pltpu.VMEM((2, PATCH, rows * cols * 2), BF16),
            pltpu.VMEM((2, TAPS * CH, PAIR), F32),
            pltpu.VMEM((2, n_ha, first_pad, 128), BF16),
            pltpu.VMEM((2, n_ha, first_pad, 128), BF16),
            pltpu.VMEM((first_pad, 128), F32),
            pltpu.VMEM((n_wa, 2, span, 128), F32),
            pltpu.VMEM((n_wa, 2, span, 128), F32),
            dma((4,)),
            dma((2, 10)),
            dma((2, 10)),
            dma((2, n_ha)),
            dma((2, n_ha)),
            dma((n_wa,)),
            dma((n_wa,)),
        ],
        compiler_params=pltpu.CompilerParams(
            collective_id=0, has_side_effects=True, vmem_limit_bytes=65024 * 1024
        ),
    )(inputs, grad_out, kernel_one, kernel_two)
    return pl.pallas_call(
        functools.partial(finish, sizes),
        out_shape=(
            jax.ShapeDtypeStruct((rows, cols, LANES), BF16),
            jax.ShapeDtypeStruct((exact,), F32),
            jax.ShapeDtypeStruct((exact,), F32),
        ),
        in_specs=[vmem_spec, vmem_spec],
        out_specs=(any_spec, vmem_spec, vmem_spec),
        scratch_shapes=[dma],
        compiler_params=pltpu.CompilerParams(vmem_limit_bytes=8 * 1024 * 1024),
    )(grad_inputs, fin)


def solution(mesh):
    n_ha, n_wa = mesh.shape["ha"], mesh.shape["wa"]

    def step(inputs, grad_out, kernel_one, kernel_two):
        rows, cols, _ = inputs.shape
        return shards((n_ha, n_wa, rows, cols), inputs, grad_out, kernel_one, kernel_two)

    return jax.shard_map(
        step,
        mesh=mesh,
        in_specs=(P("ha", "wa", None), P("ha", "wa", None), P(), P()),
        out_specs=(P("ha", "wa", None), P(("ha", "wa")), P(("ha", "wa"))),
        check_vma=False,
    )
```

```python
import functools

import jax
import jax.numpy as jnp
from jax import lax
from jax.experimental import pallas as pl
from jax.experimental.pallas import tpu as pltpu
from jax.sharding import PartitionSpec as P

CH = 64
DEPTH = 8
TAPS = 27
LANES = DEPTH * CH
PADDED = LANES + 2 * CH
PAIR = 2 * CH
PATCH = 4 * CH
KTOTAL = 3 * 16 * CH
MESH = pl.DeviceIdType.MESH
F32 = jnp.float32
BF16 = jnp.bfloat16

root_half = 0.7071067811865476
inv_root_two_pi = 0.3989422804014327


def round_up(value, multiple):
    return -(-value // multiple) * multiple


def kernel(
    sizes,
    x_hbm,
    g_hbm,
    k1_hbm,
    k2_hbm,
    gi_ref,
    fin_ref,
    xl,
    gl,
    kraw,
    kd,
    w1,
    w2,
    w3,
    esend,
    erecv,
    rowbuf,
    shifted,
    gpl,
    slopes,
    turned,
    sums,
    piece,
    got,
    along,
    along_got,
    total,
    window,
    wgot,
    local_sem,
    halo_send,
    halo_recv,
    core_send,
    core_recv,
    z_send,
    z_recv,
    last_send,
    last_recv,
):
    n_ha, n_wa, rows, cols = sizes
    ha = lax.axis_index("ha")
    wa = lax.axis_index("wa")
    pairs = rows // 2
    rows_first = (TAPS * CH) // (2 * n_ha)
    exact = (TAPS * CH * CH) // (n_ha * n_wa)

    def wrap(value, size):
        value = jnp.where(value >= size, value - size, value)
        return jnp.where(value < 0, value + size, value)

    def ha_at(step):
        return wrap(ha + step, n_ha)

    def wa_at(step):
        return wrap(wa + step, n_wa)

    n_z = n_ha // 4
    core = lax.rem(ha, 2)
    upper = lax.rem(lax.div(ha, 2), 2)
    z_here = lax.div(ha, 4)
    other_core = ha + 1 - 2 * core
    other_upper = ha + 2 - 4 * upper

    barrier = pltpu.get_barrier_semaphore()
    peers = [(ha_at(a), wa) for a in (-1, 1)]
    peers += [(ha_at(a), wa_at(b)) for a in (-1, 1) for b in (-1, 1)]
    peers += [(ha, wa_at(d)) for d in range(1, n_wa)]
    peers += [(other_upper, wa_at(d)) for d in range(n_wa)]
    peers += [(ha_at(4 * d), wa) for d in range(1, n_z)]
    loads = [
        pltpu.make_async_copy(x_hbm, xl, local_sem.at[2]),
        pltpu.make_async_copy(g_hbm, gl, local_sem.at[3]),
        pltpu.make_async_copy(k1_hbm, kraw.at[0], local_sem.at[0]),
        pltpu.make_async_copy(k2_hbm, kraw.at[1], local_sem.at[1]),
    ]
    for load in loads:
        load.start()
    for peer in peers:
        pl.semaphore_signal(barrier, inc=1, device_id=peer, device_id_type=MESH)

    sent = []

    def edges(field_refs, side):
        start, pick = (0, 0) if side == 0 else (cols - 16, 15)
        ids = lax.broadcasted_iota(jnp.int32, (16, LANES), 0)
        value = jnp.zeros((16, LANES), F32)
        for f, ref in enumerate(field_refs):
            for h in range(rows):
                block = ref[h, start : start + 16, :].astype(F32)
                cell = jnp.broadcast_to(block[pick : pick + 1], (16, LANES))
                value = jnp.where(ids == f * 8 + h, cell, value)
        return value.astype(BF16)

    def exchange(phase, field_refs):
        rows_of = []
        for f, ref in enumerate(field_refs):
            slot = phase * 2 + f
            group = []
            for side, row, step in ((0, rows - 1, 1), (1, 0, -1)):
                group.append(
                    pltpu.make_async_remote_copy(
                        src_ref=ref.at[row],
                        dst_ref=rowbuf.at[slot, side],
                        send_sem=halo_send.at[phase, f * 2 + side],
                        recv_sem=halo_recv.at[phase, f * 2 + side],
                        device_id=(ha_at(step), wa),
                        device_id_type=MESH,
                    )
                )
            rows_of.append(group)
        corners = []
        for side, wa_step in ((0, -1), (1, 1)):
            for dh in (-1, 0, 1):
                slot = (1 - side) * 3 + 1 - dh
                corners.append(
                    pltpu.make_async_remote_copy(
                        src_ref=esend.at[phase, side],
                        dst_ref=erecv.at[phase, slot],
                        send_sem=halo_send.at[phase, 4 + slot],
                        recv_sem=halo_recv.at[phase, 4 + slot],
                        device_id=(ha_at(dh), wa_at(wa_step)),
                        device_id_type=MESH,
                    )
                )
        for copy in rows_of[0] + corners:
            copy.start()
        for group in rows_of[1:]:
            for copy in group:
                copy.start()
        sent.extend(corners)
        for group in rows_of:
            sent.extend(group)
        return corners, rows_of

    def widen(value):
        zeros = jnp.zeros((value.shape[0], PADDED - LANES), F32)
        return pltpu.roll(jnp.concatenate([value, zeros], axis=1), CH, 1)

    low_ok = ha > 0
    high_ok = ha < n_ha - 1
    left_ok = wa > 0
    right_ok = wa < n_wa - 1
    cell_ids = lax.broadcasted_iota(jnp.int32, (cols, PADDED), 0)
    tile_ids = lax.broadcasted_iota(jnp.int32, (16, PADDED), 0)

    def own_rows(ref, dst):
        for h in range(rows):
            value = widen(ref[h].astype(F32))
            shifted[dst, 0, h + 1] = pltpu.roll(value, 1, 0).astype(BF16)
            shifted[dst, 1, h + 1] = value.astype(BF16)
            shifted[dst, 2, h + 1] = pltpu.roll(value, cols - 1, 0).astype(BF16)

    def finish_rows(phase, f, dst):
        slot = phase * 2 + f
        oks = (low_ok, None, high_ok)
        halo_cells = []
        for side, ok in ((0, left_ok), (1, right_ok)):
            group = []
            for r in range(3):
                value = widen(erecv[phase, side * 3 + r].astype(F32))
                good = ok if oks[r] is None else jnp.logical_and(ok, oks[r])
                group.append(jnp.where(good, value, 0.0))
            halo_cells.append(group)
        for h in range(rows):
            left = halo_cells[0][1][f * 8 + h : f * 8 + h + 1]
            right = halo_cells[1][1][f * 8 + h : f * 8 + h + 1]
            tile = shifted[dst, 0, h + 1, 0:16, :].astype(F32)
            tile = jnp.where(tile_ids == 0, jnp.broadcast_to(left, (16, PADDED)), tile)
            shifted[dst, 0, h + 1, 0:16, :] = tile.astype(BF16)
            tile = shifted[dst, 2, h + 1, cols - 16 : cols, :].astype(F32)
            tile = jnp.where(tile_ids == 15, jnp.broadcast_to(right, (16, PADDED)), tile)
            shifted[dst, 2, h + 1, cols - 16 : cols, :] = tile.astype(BF16)
        for e, side, ok, r, h in ((0, 0, low_ok, 0, rows - 1), (rows + 1, 1, high_ok, 2, 0)):
            value = widen(jnp.where(ok, rowbuf[slot, side].astype(F32), 0.0))
            left = halo_cells[0][r][f * 8 + h : f * 8 + h + 1]
            right = halo_cells[1][r][f * 8 + h : f * 8 + h + 1]
            before = jnp.where(
                cell_ids == 0,
                jnp.broadcast_to(left, (cols, PADDED)),
                pltpu.roll(value, 1, 0),
            )
            after = jnp.where(
                cell_ids == cols - 1,
                jnp.broadcast_to(right, (cols, PADDED)),
                pltpu.roll(value, cols - 1, 0),
            )
            shifted[dst, 0, e] = before.astype(BF16)
            shifted[dst, 1, e] = value.astype(BF16)
            shifted[dst, 2, e] = after.astype(BF16)

    lane_low = lax.broadcasted_iota(jnp.int32, (CH, PAIR), 1) < CH
    zero_block = jnp.zeros((CH, PAIR), BF16)

    def double():
        @pl.loop(0, 9)
        def _(ab):
            for c in range(3):
                for which in range(2):
                    block = kraw[which, ab * 3 + c]
                    kd[which, ab * 3 + c] = jnp.concatenate([block, block], axis=1)

    def tap_block(which, index, c):
        return kd[which, index(c)] if 0 <= c <= 2 else zero_block

    def build_rows(which, dst):
        @pl.loop(0, 3)
        def _(b):
            base = b * 16 * CH
            for di in range(4):
                for a in range(4):
                    if a < 3:
                        index = lambda c: 9 * a + 3 * b + c
                        tile = jnp.where(
                            lane_low,
                            tap_block(which, index, di),
                            tap_block(which, index, di - 1),
                        )
                    else:
                        tile = zero_block
                    here = pl.multiple_of(base + (a * 4 + di) * CH, CH)
                    dst[pl.ds(here, CH), 0:PAIR] = tile
                    here = pl.multiple_of(base + ((a + 1) % 4 * 4 + di) * CH, CH)
                    dst[pl.ds(here, CH), PAIR : 2 * PAIR] = tile

    def build_turned(which, dst):
        @pl.loop(0, 3)
        def _(b):
            base = b * 16 * CH
            for dd in range(2):
                for m in range(2):
                    for a in range(4):
                        if a < 3:
                            index = lambda c: TAPS - 1 - (9 * a + 3 * b + c)
                            tile = jnp.where(
                                lane_low,
                                tap_block(which, index, 2 * m - dd),
                                tap_block(which, index, 2 * m + 1 - dd),
                            )
                        else:
                            tile = zero_block
                        here = pl.multiple_of(base + (a * 4 + 2 * m) * CH, 128)
                        dst[dd * CH : (dd + 1) * CH, pl.ds(here, PAIR)] = tile
                        here = pl.multiple_of(base + ((a + 1) % 4 * 4 + 2 * m) * CH, 128)
                        dst[PAIR + dd * CH : PAIR + (dd + 1) * CH, pl.ds(here, PAIR)] = tile

    loads[0].wait()
    loads[1].wait()
    for side in range(2):
        esend[0, side] = edges((xl, gl), side)
    pl.semaphore_wait(barrier, len(peers))
    corners, row_copies = exchange(0, (xl, gl))

    loads[2].wait()
    loads[3].wait()
    double()
    build_rows(0, w1)
    build_turned(1, w2)
    build_turned(0, w3)
    own_rows(xl, 0)
    own_rows(gl, 1)

    for copy in corners + row_copies[0]:
        copy.wait_recv()
    finish_rows(0, 0, 0)

    def patches(src, b, i, hp):
        return jnp.concatenate(
            [
                shifted[src, b, 2 * hp + i, :, dp * PAIR : dp * PAIR + PATCH]
                for dp in range(DEPTH // 2)
            ],
            axis=0,
        )

    def conv(src, hp, weights, flipped):
        left = jnp.concatenate(
            [patches(src, b, i, hp) for b in range(3) for i in range(4)], axis=1
        )
        dims = (((1,), (1,)), ((), ())) if flipped else (((1,), (0,)), ((), ()))
        return lax.dot_general(left, weights[...], dims, preferred_element_type=F32)

    def spread(dst, hp, value):
        for hh in range(2):
            for dp in range(DEPTH // 2):
                dst[2 * hp + hh, :, dp * PAIR : (dp + 1) * PAIR] = value[
                    dp * cols : (dp + 1) * cols, hh * PAIR : (hh + 1) * PAIR
                ]

    block = cols * (DEPTH // 2)
    for hp in range(pairs):
        pre = conv(0, hp, w1, False)
        phi = 0.5 * (1.0 + lax.erf(pre * root_half))
        turned[1, :, hp * block : (hp + 1) * block] = (pre * phi).astype(BF16).T
        slopes[hp] = phi + pre * inv_root_two_pi * jnp.exp(-0.5 * pre * pre)
    for copy in row_copies[1]:
        copy.wait_recv()
    finish_rows(0, 1, 1)
    for hp in range(pairs):
        grad_pre = (conv(1, hp, w2, True) * slopes[hp]).astype(BF16)
        spread(gpl, hp, grad_pre)
        turned[0, :, hp * block : (hp + 1) * block] = grad_pre.T

    for side in range(2):
        esend[1, side] = edges((gpl,), side)
    corners, row_copies = exchange(1, (gpl,))

    half = lax.broadcasted_iota(jnp.int32, (CH, PAIR), 1) < CH

    def gradients(src, b):
        blocks = []
        for i in range(4):
            right = jnp.concatenate([patches(src, b, i, hp) for hp in range(pairs)], axis=0)
            blocks.append(
                lax.dot_general(
                    turned[src],
                    right,
                    (((1,), (0,)), ((), ())),
                    preferred_element_type=F32,
                )
            )
        for a in range(3):
            low, high = blocks[a], blocks[a + 1]
            even = low[0:CH] + high[PAIR : PAIR + CH]
            odd = low[CH:PAIR] + high[PAIR + CH : 2 * PAIR]
            yield a, even[:, :PAIR], even[:, PAIR:], odd[:, :PAIR], odd[:, PAIR:]

    def send_to_core(which):
        for j in range(n_ha):
            first = sums[which, pl.ds(2 * j * rows_first, rows_first, stride=2), :]
            second = sums[which, pl.ds(2 * j * rows_first + 1, rows_first, stride=2), :]
            value = jnp.where(
                lax.broadcasted_iota(jnp.int32, (rows_first, PAIR), 1) < CH,
                first,
                pltpu.roll(second, CH, 1),
            )
            piece[which, j % 2, j // 2, 0:rows_first, :] = value.astype(BF16)
        copy = pltpu.make_async_remote_copy(
            src_ref=piece.at[which, 1 - core],
            dst_ref=got.at[which],
            send_sem=core_send.at[which],
            recv_sem=core_recv.at[which],
            device_id=(other_core, wa),
            device_id_type=MESH,
        )
        copy.start()
        sent.append(copy)
        return copy

    def send_along_z(which, arrival):
        arrival.wait_recv()
        for t in range(n_ha // 2):
            value = piece[which, core, t].astype(F32) + got[which, t].astype(F32)
            along[which, t // 2, t % 2] = value.astype(BF16)
        copies = []
        for d in range(1, n_z):
            copies.append(
                pltpu.make_async_remote_copy(
                    src_ref=along.at[which, wrap(z_here + d, n_z)],
                    dst_ref=along_got.at[which, d],
                    send_sem=z_send.at[which, d],
                    recv_sem=z_recv.at[which, d],
                    device_id=(ha_at(4 * d), wa),
                    device_id_type=MESH,
                )
            )
        for copy in copies:
            copy.start()
        sent.extend(copies)
        return copies

    for b in range(3):
        for a, even0, even1, odd0, odd1 in gradients(1, b):
            turn = pltpu.roll(odd1, CH, 1)
            values = (even0 + pltpu.roll(odd0, CH, 1), odd1 + pltpu.roll(even0, CH, 1), even1 + turn)
            for c in range(3):
                start = (TAPS - 1 - (9 * a + 3 * b + c)) * CH
                sums[1, start : start + CH, :] = values[c]
    arrivals = [None, send_to_core(1)]
    z_copies = [None, None]
    for b in range(3):
        for a, even0, even1, odd0, odd1 in gradients(0, b):
            turn = pltpu.roll(odd1, CH, 1)
            both = even0 + jnp.where(half, pltpu.roll(odd0, CH, 1), turn)
            start = (9 * a + 3 * b) * CH
            sums[0, start : start + 2 * CH, 0:CH] = both.T
            sums[0, start + 2 * CH : start + 3 * CH, 0:CH] = (even1 + turn).T[0:CH]
        if b == 1:
            z_copies[1] = send_along_z(1, arrivals[1])
    arrivals[0] = send_to_core(0)

    own_rows(gpl, 2)
    z_copies[0] = send_along_z(0, arrivals[0])
    for copy in corners + row_copies[0]:
        copy.wait_recv()
    finish_rows(1, 0, 2)
    for hp in range(pairs):
        spread(gi_ref, hp, conv(2, hp, w3, True).astype(BF16))

    starts = [(k * rows_first) // n_wa for k in range(n_wa)]
    span = window.shape[3]
    for which in (1, 0):
        for copy in z_copies[which]:
            copy.wait_recv()
        for u in range(2):
            value = along[which, z_here, u].astype(F32)
            for d in range(1, n_z):
                value += along_got[which, d, u].astype(F32)
            total[which, u] = value
            for k in range(n_wa):
                window[u, k, which] = total[which, u, starts[k] : starts[k] + span, :]
    lasts = []
    for step in range(2):
        up = upper if step == 0 else 1 - upper
        for d in range(n_wa):
            if step == 0 and d == 0:
                continue
            to = wa_at(d)
            lasts.append(
                pltpu.make_async_remote_copy(
                    src_ref=window.at[up, to],
                    dst_ref=wgot.at[step, d],
                    send_sem=last_send.at[step, d],
                    recv_sem=last_recv.at[step, d],
                    device_id=(ha if step == 0 else other_upper, to),
                    device_id_type=MESH,
                )
            )
    for copy in lasts:
        copy.start()
    for copy in lasts:
        copy.wait_recv()
    value = window[upper, wa]
    for step in range(2):
        for d in range(n_wa):
            if step or d:
                value += wgot[step, d]
    fin_ref[...] = value
    for copy in sent + lasts:
        copy.wait_send()


def finish(sizes, gi_ref, fin_ref, gi_hbm, one_ref, two_ref, sem):
    n_ha, n_wa, rows, cols = sizes
    wa = lax.axis_index("wa")
    exact = (TAPS * CH * CH) // (n_ha * n_wa)
    store = pltpu.make_async_copy(gi_ref, gi_hbm, sem)
    store.start()
    offset = lax.rem(wa * exact, 128)
    count = -(-exact // 128)
    lanes = lax.broadcasted_iota(jnp.int32, (count, 128), 1)
    for which, out in ((0, one_ref), (1, two_ref)):
        value = pltpu.roll(fin_ref[which], 128 - offset, 1)
        value = jnp.where(lanes < 128 - offset, value[0:count], value[1 : count + 1])
        for r in range(count):
            width = min(128, exact - r * 128)
            out[pl.ds(r * 128, width)] = value[r, 0:width]
    store.wait()


def shards(sizes, inputs, grad_out, kernel_one, kernel_two):
    n_ha, n_wa, rows, cols = sizes
    rows_first = (TAPS * CH) // (2 * n_ha)
    exact = (TAPS * CH * CH) // (n_ha * n_wa)
    out_rows = -(-exact // 128)
    span = round_up(out_rows + 1, 8)
    first_pad = round_up(max(rows_first, (n_wa - 1) * rows_first // n_wa + span), 16)
    any_spec = pl.BlockSpec(memory_space=pl.ANY)
    vmem_spec = pl.BlockSpec(memory_space=pltpu.VMEM)
    dma = pltpu.SemaphoreType.DMA
    grad_inputs, fin = pl.pallas_call(
        functools.partial(kernel, sizes),
        out_shape=(
            pltpu.VMEM((rows, cols, LANES), BF16),
            pltpu.VMEM((2, span, 128), F32),
        ),
        in_specs=[pl.BlockSpec(memory_space=pltpu.HBM)] * 4,
        out_specs=(vmem_spec, vmem_spec),
        scratch_shapes=[
            pltpu.VMEM((rows, cols, LANES), BF16),
            pltpu.VMEM((rows, cols, LANES), BF16),
            pltpu.VMEM((2, TAPS, CH, CH), BF16),
            pltpu.VMEM((2, TAPS, CH, PAIR), BF16),
            pltpu.VMEM((KTOTAL, PATCH), BF16),
            pltpu.VMEM((PATCH, KTOTAL), BF16),
            pltpu.VMEM((PATCH, KTOTAL), BF16),
            pltpu.VMEM((2, 2, 16, LANES), BF16),
            pltpu.VMEM((2, 6, 16, LANES), BF16),
            pltpu.VMEM((3, 2, cols, LANES), BF16),
            pltpu.VMEM((3, 3, rows + 2, cols, PADDED), BF16),
            pltpu.VMEM((rows, cols, LANES), BF16),
            pltpu.VMEM((rows // 2, cols * DEPTH // 2, PATCH), F32),
            pltpu.VMEM((2, PATCH, rows * cols * 2), BF16),
            pltpu.VMEM((2, TAPS * CH, PAIR), F32),
            pltpu.VMEM((2, 2, n_ha // 2, first_pad, 128), BF16),
            pltpu.VMEM((2, n_ha // 2, first_pad, 128), BF16),
            pltpu.VMEM((2, n_ha // 4, 2, first_pad, 128), BF16),
            pltpu.VMEM((2, n_ha // 4, 2, first_pad, 128), BF16),
            pltpu.VMEM((2, 2, first_pad, 128), F32),
            pltpu.VMEM((2, n_wa, 2, span, 128), F32),
            pltpu.VMEM((2, n_wa, 2, span, 128), F32),
            dma((4,)),
            dma((2, 10)),
            dma((2, 10)),
            dma((2,)),
            dma((2,)),
            dma((2, n_ha // 4)),
            dma((2, n_ha // 4)),
            dma((2, n_wa)),
            dma((2, n_wa)),
        ],
        compiler_params=pltpu.CompilerParams(
            collective_id=0, has_side_effects=True, vmem_limit_bytes=65024 * 1024
        ),
    )(inputs, grad_out, kernel_one, kernel_two)
    return pl.pallas_call(
        functools.partial(finish, sizes),
        out_shape=(
            jax.ShapeDtypeStruct((rows, cols, LANES), BF16),
            jax.ShapeDtypeStruct((exact,), F32),
            jax.ShapeDtypeStruct((exact,), F32),
        ),
        in_specs=[vmem_spec, vmem_spec],
        out_specs=(any_spec, vmem_spec, vmem_spec),
        scratch_shapes=[dma],
        compiler_params=pltpu.CompilerParams(vmem_limit_bytes=8 * 1024 * 1024),
    )(grad_inputs, fin)


def solution(mesh):
    n_ha, n_wa = mesh.shape["ha"], mesh.shape["wa"]

    def step(inputs, grad_out, kernel_one, kernel_two):
        rows, cols, _ = inputs.shape
        return shards((n_ha, n_wa, rows, cols), inputs, grad_out, kernel_one, kernel_two)

    return jax.shard_map(
        step,
        mesh=mesh,
        in_specs=(P("ha", "wa", None), P("ha", "wa", None), P(), P()),
        out_specs=(P("ha", "wa", None), P(("ha", "wa")), P(("ha", "wa"))),
        check_vma=False,
    )
```

```python
import functools

import jax
import jax.numpy as jnp
from jax import lax
from jax.experimental import pallas as pl
from jax.experimental.pallas import tpu as pltpu
from jax.sharding import PartitionSpec as P

CH = 64
DEPTH = 8
TAPS = 27
LANES = DEPTH * CH
PADDED = LANES + 2 * CH
PAIR = 2 * CH
PATCH = 4 * CH
KTOTAL = 3 * 16 * CH
MESH = pl.DeviceIdType.MESH
SENT_AFTER = 0
F32 = jnp.float32
BF16 = jnp.bfloat16

root_half = 0.7071067811865476
inv_root_two_pi = 0.3989422804014327


def round_up(value, multiple):
    return -(-value // multiple) * multiple


def kernel(
    sizes,
    x_hbm,
    g_hbm,
    k1_hbm,
    k2_hbm,
    gi_ref,
    fin_ref,
    xl,
    gl,
    kraw,
    kd,
    w1,
    w2,
    w3,
    esend,
    erecv,
    rowbuf,
    shifted,
    gpl,
    held,
    turned,
    sums,
    piece,
    got,
    along,
    along_got,
    total,
    window,
    wgot,
    local_sem,
    halo_send,
    halo_recv,
    core_send,
    core_recv,
    z_send,
    z_recv,
    last_send,
    last_recv,
):
    n_ha, n_wa, rows, cols = sizes
    ha = lax.axis_index("ha")
    wa = lax.axis_index("wa")
    pairs = rows // 2
    rows_first = (TAPS * CH) // (2 * n_ha)
    exact = (TAPS * CH * CH) // (n_ha * n_wa)

    def wrap(value, size):
        value = jnp.where(value >= size, value - size, value)
        return jnp.where(value < 0, value + size, value)

    def ha_at(step):
        return wrap(ha + step, n_ha)

    def wa_at(step):
        return wrap(wa + step, n_wa)

    n_z = n_ha // 4
    core = lax.rem(ha, 2)
    upper = lax.rem(lax.div(ha, 2), 2)
    z_here = lax.div(ha, 4)
    other_core = ha + 1 - 2 * core
    other_upper = ha + 2 - 4 * upper

    barrier = pltpu.get_barrier_semaphore()
    peers = [(ha_at(a), wa) for a in (-1, 1)]
    peers += [(ha, wa_at(d)) for d in (-1, 1)[: n_wa - 1]]
    peers += [(ha_at(a), wa_at(b)) for a in (-1, 1) for b in (-1, 1)]
    peers += [(ha, wa_at(d)) for d in range(2, n_wa - 1)]
    peers += [(other_upper, wa_at(d)) for d in range(n_wa)]
    peers += [(ha_at(4 * d), wa) for d in range(1, n_z)]
    loads = [
        pltpu.make_async_copy(x_hbm, xl, local_sem.at[2]),
        pltpu.make_async_copy(g_hbm, gl, local_sem.at[3]),
        pltpu.make_async_copy(k1_hbm, kraw.at[0], local_sem.at[0]),
        pltpu.make_async_copy(k2_hbm, kraw.at[1], local_sem.at[1]),
    ]
    for peer in peers[:8]:
        pl.semaphore_signal(barrier, inc=1, device_id=peer, device_id_type=MESH)
    for load in loads:
        load.start()
    for peer in peers[8:]:
        pl.semaphore_signal(barrier, inc=1, device_id=peer, device_id_type=MESH)

    sent = []

    def edges(field_refs, side):
        start, pick = (0, 0) if side == 0 else (cols - 16, 15)
        ids = lax.broadcasted_iota(jnp.int32, (16, LANES), 0)
        value = jnp.zeros((16, LANES), F32)
        for f, ref in enumerate(field_refs):
            for h in range(rows):
                block = ref[h, start : start + 16, :].astype(F32)
                cell = jnp.broadcast_to(block[pick : pick + 1], (16, LANES))
                value = jnp.where(ids == f * 8 + h, cell, value)
        return value.astype(BF16)

    def exchange(phase, field_refs):
        rows_of = []
        for f, ref in enumerate(field_refs):
            slot = phase * 2 + f
            group = []
            for side, row, step in ((0, rows - 1, 1), (1, 0, -1)):
                group.append(
                    pltpu.make_async_remote_copy(
                        src_ref=ref.at[row],
                        dst_ref=rowbuf.at[slot, side],
                        send_sem=halo_send.at[phase, f * 2 + side],
                        recv_sem=halo_recv.at[phase, f * 2 + side],
                        device_id=(ha_at(step), wa),
                        device_id_type=MESH,
                    )
                )
            rows_of.append(group)
        corners = []
        for side, wa_step in ((0, -1), (1, 1)):
            for dh in (-1, 0, 1):
                slot = (1 - side) * 3 + 1 - dh
                corners.append(
                    pltpu.make_async_remote_copy(
                        src_ref=esend.at[phase, side],
                        dst_ref=erecv.at[phase, slot],
                        send_sem=halo_send.at[phase, 4 + slot],
                        recv_sem=halo_recv.at[phase, 4 + slot],
                        device_id=(ha_at(dh), wa_at(wa_step)),
                        device_id_type=MESH,
                    )
                )
        beside = [corners[1], corners[4]]
        corners = [corners[i] for i in (0, 2, 3, 5)]
        for group in [beside, rows_of[0], corners] + rows_of[1:]:
            for copy in group:
                copy.start()
            sent.extend(group)
        return beside, corners, rows_of

    def widen(value):
        zeros = jnp.zeros((value.shape[0], PADDED - LANES), F32)
        return pltpu.roll(jnp.concatenate([value, zeros], axis=1), CH, 1)

    low_ok = ha > 0
    high_ok = ha < n_ha - 1
    left_ok = wa > 0
    right_ok = wa < n_wa - 1
    cell_ids = lax.broadcasted_iota(jnp.int32, (cols, PADDED), 0)
    tile_ids = lax.broadcasted_iota(jnp.int32, (16, PADDED), 0)

    def own_rows(ref, dst):
        for h in range(rows):
            value = widen(ref[h].astype(F32))
            shifted[dst, 0, h + 1] = pltpu.roll(value, 1, 0).astype(BF16)
            shifted[dst, 1, h + 1] = value.astype(BF16)
            shifted[dst, 2, h + 1] = pltpu.roll(value, cols - 1, 0).astype(BF16)

    def halo_cells(phase, side, r):
        ok = (left_ok, right_ok)[side]
        if r != 1:
            ok = jnp.logical_and(ok, (low_ok, None, high_ok)[r])
        return jnp.where(ok, widen(erecv[phase, side * 3 + r].astype(F32)), 0.0)

    def finish_own(phase, f, dst):
        sides = [halo_cells(phase, side, 1) for side in range(2)]
        for h in range(rows):
            left = sides[0][f * 8 + h : f * 8 + h + 1]
            right = sides[1][f * 8 + h : f * 8 + h + 1]
            tile = shifted[dst, 0, h + 1, 0:16, :].astype(F32)
            tile = jnp.where(tile_ids == 0, jnp.broadcast_to(left, (16, PADDED)), tile)
            shifted[dst, 0, h + 1, 0:16, :] = tile.astype(BF16)
            tile = shifted[dst, 2, h + 1, cols - 16 : cols, :].astype(F32)
            tile = jnp.where(tile_ids == 15, jnp.broadcast_to(right, (16, PADDED)), tile)
            shifted[dst, 2, h + 1, cols - 16 : cols, :] = tile.astype(BF16)

    def outer_rows(phase, f, dst):
        slot = phase * 2 + f
        for e, side, ok, r, h in ((0, 0, low_ok, 0, rows - 1), (rows + 1, 1, high_ok, 2, 0)):
            value = widen(jnp.where(ok, rowbuf[slot, side].astype(F32), 0.0))
            left = halo_cells(phase, 0, r)[f * 8 + h : f * 8 + h + 1]
            right = halo_cells(phase, 1, r)[f * 8 + h : f * 8 + h + 1]
            before = jnp.where(
                cell_ids == 0,
                jnp.broadcast_to(left, (cols, PADDED)),
                pltpu.roll(value, 1, 0),
            )
            after = jnp.where(
                cell_ids == cols - 1,
                jnp.broadcast_to(right, (cols, PADDED)),
                pltpu.roll(value, cols - 1, 0),
            )
            shifted[dst, 0, e] = before.astype(BF16)
            shifted[dst, 1, e] = value.astype(BF16)
            shifted[dst, 2, e] = after.astype(BF16)

    lane_low = lax.broadcasted_iota(jnp.int32, (CH, PAIR), 1) < CH
    zero_block = jnp.zeros((CH, PAIR), BF16)

    def double():
        @pl.loop(0, 9)
        def _(ab):
            for c in range(3):
                for which in range(2):
                    block = kraw[which, ab * 3 + c]
                    kd[which, ab * 3 + c] = jnp.concatenate([block, block], axis=1)

    def tap_block(which, index, c):
        return kd[which, index(c)] if 0 <= c <= 2 else zero_block

    def build_rows(which, dst):
        @pl.loop(0, 3)
        def _(b):
            base = b * 16 * CH
            for di in range(4):
                for a in range(4):
                    if a < 3:
                        index = lambda c: 9 * a + 3 * b + c
                        tile = jnp.where(
                            lane_low,
                            tap_block(which, index, di),
                            tap_block(which, index, di - 1),
                        )
                    else:
                        tile = zero_block
                    here = pl.multiple_of(base + (a * 4 + di) * CH, CH)
                    dst[pl.ds(here, CH), 0:PAIR] = tile
                    here = pl.multiple_of(base + ((a + 1) % 4 * 4 + di) * CH, CH)
                    dst[pl.ds(here, CH), PAIR : 2 * PAIR] = tile

    def build_turned(which, dst):
        @pl.loop(0, 3)
        def _(b):
            base = b * 16 * CH
            for dd in range(2):
                for m in range(2):
                    for a in range(4):
                        if a < 3:
                            index = lambda c: TAPS - 1 - (9 * a + 3 * b + c)
                            tile = jnp.where(
                                lane_low,
                                tap_block(which, index, 2 * m - dd),
                                tap_block(which, index, 2 * m + 1 - dd),
                            )
                        else:
                            tile = zero_block
                        here = pl.multiple_of(base + (a * 4 + 2 * m) * CH, 128)
                        dst[dd * CH : (dd + 1) * CH, pl.ds(here, PAIR)] = tile
                        here = pl.multiple_of(base + ((a + 1) % 4 * 4 + 2 * m) * CH, 128)
                        dst[PAIR + dd * CH : PAIR + (dd + 1) * CH, pl.ds(here, PAIR)] = tile

    loads[0].wait()
    loads[1].wait()
    for side in range(2):
        esend[0, side] = edges((xl, gl), side)
    pl.semaphore_wait(barrier, len(peers))
    beside, corners, row_copies = exchange(0, (xl, gl))

    loads[2].wait()
    loads[3].wait()
    double()
    build_rows(0, w1)
    build_turned(1, w2)
    build_turned(0, w3)
    own_rows(xl, 0)
    own_rows(gl, 1)

    for copy in beside:
        copy.wait_recv()
    finish_own(0, 0, 0)
    finish_own(0, 1, 1)

    def patches(src, b, i, hp):
        return jnp.concatenate(
            [
                shifted[src, b, 2 * hp + i, :, dp * PAIR : dp * PAIR + PATCH]
                for dp in range(DEPTH // 2)
            ],
            axis=0,
        )

    def inner(hp):
        return [i for i in range(4) if 0 < 2 * hp + i < rows + 1]

    def outer(hp):
        return [i for i in range(4) if i not in inner(hp)]

    def conv(src, hp, weights, flipped, window_rows):
        spots = [(b, i) for b in range(3) for i in window_rows]
        left = jnp.concatenate([patches(src, b, i, hp) for b, i in spots], axis=1)
        parts = [slice((b * 4 + i) * PATCH, (b * 4 + i + 1) * PATCH) for b, i in spots]
        if flipped:
            right = jnp.concatenate([weights[:, part] for part in parts], axis=1)
            dims = (((1,), (1,)), ((), ()))
        else:
            right = jnp.concatenate([weights[part, :] for part in parts], axis=0)
            dims = (((1,), (0,)), ((), ()))
        return lax.dot_general(left, right, dims, preferred_element_type=F32)

    def spread(dst, hp, value):
        for hh in range(2):
            for dp in range(DEPTH // 2):
                dst[2 * hp + hh, :, dp * PAIR : (dp + 1) * PAIR] = value[
                    dp * cols : (dp + 1) * cols, hh * PAIR : (hh + 1) * PAIR
                ]

    block = cols * (DEPTH // 2)
    for hp in range(pairs):
        held[0, hp] = conv(0, hp, w1, False, inner(hp))
        held[1, hp] = conv(1, hp, w2, True, inner(hp))
    for copy in row_copies[0] + corners:
        copy.wait_recv()
    outer_rows(0, 0, 0)
    for hp in range(pairs):
        pre = held[0, hp] + conv(0, hp, w1, False, outer(hp))
        phi = 0.5 * (1.0 + lax.erf(pre * root_half))
        turned[1, :, hp * block : (hp + 1) * block] = (pre * phi).astype(BF16).T
        held[0, hp] = phi + pre * inv_root_two_pi * jnp.exp(-0.5 * pre * pre)
    for copy in row_copies[1]:
        copy.wait_recv()
    outer_rows(0, 1, 1)
    for hp in range(pairs):
        grad_active = held[1, hp] + conv(1, hp, w2, True, outer(hp))
        grad_pre = (grad_active * held[0, hp]).astype(BF16)
        spread(gpl, hp, grad_pre)
        turned[0, :, hp * block : (hp + 1) * block] = grad_pre.T

    half = lax.broadcasted_iota(jnp.int32, (CH, PAIR), 1) < CH

    def gradients(src, b):
        blocks = []
        for i in range(4):
            right = jnp.concatenate([patches(src, b, i, hp) for hp in range(pairs)], axis=0)
            blocks.append(
                lax.dot_general(
                    turned[src],
                    right,
                    (((1,), (0,)), ((), ())),
                    preferred_element_type=F32,
                )
            )
        for a in range(3):
            low, high = blocks[a], blocks[a + 1]
            even = low[0:CH] + high[PAIR : PAIR + CH]
            odd = low[CH:PAIR] + high[PAIR + CH : 2 * PAIR]
            yield a, even[:, :PAIR], even[:, PAIR:], odd[:, :PAIR], odd[:, PAIR:]

    def send_to_core(which):
        for j in range(n_ha):
            first = sums[which, pl.ds(2 * j * rows_first, rows_first, stride=2), :]
            second = sums[which, pl.ds(2 * j * rows_first + 1, rows_first, stride=2), :]
            value = jnp.where(
                lax.broadcasted_iota(jnp.int32, (rows_first, PAIR), 1) < CH,
                first,
                pltpu.roll(second, CH, 1),
            )
            piece[which, j % 2, j // 2, 0:rows_first, :] = value.astype(BF16)
        copy = pltpu.make_async_remote_copy(
            src_ref=piece.at[which, 1 - core],
            dst_ref=got.at[which],
            send_sem=core_send.at[which],
            recv_sem=core_recv.at[which],
            device_id=(other_core, wa),
            device_id_type=MESH,
        )
        copy.start()
        sent.append(copy)
        return copy

    def send_along_z(which, arrival):
        arrival.wait_recv()
        for t in range(n_ha // 2):
            value = piece[which, core, t].astype(F32) + got[which, t].astype(F32)
            along[which, t // 2, t % 2] = value.astype(BF16)
        copies = []
        for d in range(1, n_z):
            copies.append(
                pltpu.make_async_remote_copy(
                    src_ref=along.at[which, wrap(z_here + d, n_z)],
                    dst_ref=along_got.at[which, d],
                    send_sem=z_send.at[which, d],
                    recv_sem=z_recv.at[which, d],
                    device_id=(ha_at(4 * d), wa),
                    device_id_type=MESH,
                )
            )
        for copy in copies:
            copy.start()
        sent.extend(copies)
        return copies

    for b in range(3):
        for a, even0, even1, odd0, odd1 in gradients(1, b):
            turn = pltpu.roll(odd1, CH, 1)
            values = (even0 + pltpu.roll(odd0, CH, 1), odd1 + pltpu.roll(even0, CH, 1), even1 + turn)
            for c in range(3):
                start = (TAPS - 1 - (9 * a + 3 * b + c)) * CH
                sums[1, start : start + CH, :] = values[c]
        if b == SENT_AFTER:
            for side in range(2):
                esend[1, side] = edges((gpl,), side)
            beside, corners, row_copies = exchange(1, (gpl,))
    arrivals = [None, send_to_core(1)]
    z_copies = [None, None]
    for b in range(3):
        for a, even0, even1, odd0, odd1 in gradients(0, b):
            turn = pltpu.roll(odd1, CH, 1)
            both = even0 + jnp.where(half, pltpu.roll(odd0, CH, 1), turn)
            start = (9 * a + 3 * b) * CH
            sums[0, start : start + 2 * CH, 0:CH] = both.T
            sums[0, start + 2 * CH : start + 3 * CH, 0:CH] = (even1 + turn).T[0:CH]
        if b == 1:
            z_copies[1] = send_along_z(1, arrivals[1])
    arrivals[0] = send_to_core(0)

    own_rows(gpl, 2)
    z_copies[0] = send_along_z(0, arrivals[0])
    for copy in beside + corners + row_copies[0]:
        copy.wait_recv()
    finish_own(1, 0, 2)
    outer_rows(1, 0, 2)
    for hp in range(pairs):
        spread(gi_ref, hp, conv(2, hp, w3, True, range(4)).astype(BF16))

    starts = [(k * rows_first) // n_wa for k in range(n_wa)]
    span = window.shape[3]
    for which in (1, 0):
        for copy in z_copies[which]:
            copy.wait_recv()
        for u in range(2):
            value = along[which, z_here, u].astype(F32)
            for d in range(1, n_z):
                value += along_got[which, d, u].astype(F32)
            total[which, u] = value
            for k in range(n_wa):
                window[u, k, which] = total[which, u, starts[k] : starts[k] + span, :]
    lasts = []
    for step in range(2):
        up = upper if step == 0 else 1 - upper
        for d in range(n_wa):
            if step == 0 and d == 0:
                continue
            to = wa_at(d)
            lasts.append(
                pltpu.make_async_remote_copy(
                    src_ref=window.at[up, to],
                    dst_ref=wgot.at[step, d],
                    send_sem=last_send.at[step, d],
                    recv_sem=last_recv.at[step, d],
                    device_id=(ha if step == 0 else other_upper, to),
                    device_id_type=MESH,
                )
            )
    for copy in lasts:
        copy.start()
    for copy in lasts:
        copy.wait_recv()
    value = window[upper, wa]
    for step in range(2):
        for d in range(n_wa):
            if step or d:
                value += wgot[step, d]
    fin_ref[...] = value
    for copy in sent + lasts:
        copy.wait_send()


def finish(sizes, gi_ref, fin_ref, gi_hbm, one_ref, two_ref, sem):
    n_ha, n_wa, rows, cols = sizes
    wa = lax.axis_index("wa")
    exact = (TAPS * CH * CH) // (n_ha * n_wa)
    store = pltpu.make_async_copy(gi_ref, gi_hbm, sem)
    store.start()
    offset = lax.rem(wa * exact, 128)
    count = -(-exact // 128)
    lanes = lax.broadcasted_iota(jnp.int32, (count, 128), 1)
    for which, out in ((0, one_ref), (1, two_ref)):
        value = pltpu.roll(fin_ref[which], 128 - offset, 1)
        value = jnp.where(lanes < 128 - offset, value[0:count], value[1 : count + 1])
        for r in range(count):
            width = min(128, exact - r * 128)
            out[pl.ds(r * 128, width)] = value[r, 0:width]
    store.wait()


def shards(sizes, inputs, grad_out, kernel_one, kernel_two):
    n_ha, n_wa, rows, cols = sizes
    rows_first = (TAPS * CH) // (2 * n_ha)
    exact = (TAPS * CH * CH) // (n_ha * n_wa)
    out_rows = -(-exact // 128)
    span = round_up(out_rows + 1, 8)
    first_pad = round_up(max(rows_first, (n_wa - 1) * rows_first // n_wa + span), 8)
    any_spec = pl.BlockSpec(memory_space=pl.ANY)
    vmem_spec = pl.BlockSpec(memory_space=pltpu.VMEM)
    dma = pltpu.SemaphoreType.DMA
    grad_inputs, fin = pl.pallas_call(
        functools.partial(kernel, sizes),
        out_shape=(
            pltpu.VMEM((rows, cols, LANES), BF16),
            pltpu.VMEM((2, span, 128), F32),
        ),
        in_specs=[pl.BlockSpec(memory_space=pltpu.HBM)] * 4,
        out_specs=(vmem_spec, vmem_spec),
        scratch_shapes=[
            pltpu.VMEM((rows, cols, LANES), BF16),
            pltpu.VMEM((rows, cols, LANES), BF16),
            pltpu.VMEM((2, TAPS, CH, CH), BF16),
            pltpu.VMEM((2, TAPS, CH, PAIR), BF16),
            pltpu.VMEM((KTOTAL, PATCH), BF16),
            pltpu.VMEM((PATCH, KTOTAL), BF16),
            pltpu.VMEM((PATCH, KTOTAL), BF16),
            pltpu.VMEM((2, 2, 16, LANES), BF16),
            pltpu.VMEM((2, 6, 16, LANES), BF16),
            pltpu.VMEM((3, 2, cols, LANES), BF16),
            pltpu.VMEM((3, 3, rows + 2, cols, PADDED), BF16),
            pltpu.VMEM((rows, cols, LANES), BF16),
            pltpu.VMEM((2, rows // 2, cols * DEPTH // 2, PATCH), F32),
            pltpu.VMEM((2, PATCH, rows * cols * 2), BF16),
            pltpu.VMEM((2, TAPS * CH, PAIR), F32),
            pltpu.VMEM((2, 2, n_ha // 2, first_pad, 128), BF16),
            pltpu.VMEM((2, n_ha // 2, first_pad, 128), BF16),
            pltpu.VMEM((2, n_ha // 4, 2, first_pad, 128), BF16),
            pltpu.VMEM((2, n_ha // 4, 2, first_pad, 128), BF16),
            pltpu.VMEM((2, 2, first_pad, 128), F32),
            pltpu.VMEM((2, n_wa, 2, span, 128), F32),
            pltpu.VMEM((2, n_wa, 2, span, 128), F32),
            dma((4,)),
            dma((2, 10)),
            dma((2, 10)),
            dma((2,)),
            dma((2,)),
            dma((2, n_ha // 4)),
            dma((2, n_ha // 4)),
            dma((2, n_wa)),
            dma((2, n_wa)),
        ],
        compiler_params=pltpu.CompilerParams(
            collective_id=0, has_side_effects=True, vmem_limit_bytes=65024 * 1024
        ),
    )(inputs, grad_out, kernel_one, kernel_two)
    return pl.pallas_call(
        functools.partial(finish, sizes),
        out_shape=(
            jax.ShapeDtypeStruct((rows, cols, LANES), BF16),
            jax.ShapeDtypeStruct((exact,), F32),
            jax.ShapeDtypeStruct((exact,), F32),
        ),
        in_specs=[vmem_spec, vmem_spec],
        out_specs=(any_spec, vmem_spec, vmem_spec),
        scratch_shapes=[dma],
        compiler_params=pltpu.CompilerParams(vmem_limit_bytes=8 * 1024 * 1024),
    )(grad_inputs, fin)


def solution(mesh):
    n_ha, n_wa = mesh.shape["ha"], mesh.shape["wa"]

    def step(inputs, grad_out, kernel_one, kernel_two):
        rows, cols, _ = inputs.shape
        return shards((n_ha, n_wa, rows, cols), inputs, grad_out, kernel_one, kernel_two)

    return jax.shard_map(
        step,
        mesh=mesh,
        in_specs=(P("ha", "wa", None), P("ha", "wa", None), P(), P()),
        out_specs=(P("ha", "wa", None), P(("ha", "wa")), P(("ha", "wa"))),
        check_vma=False,
    )
```

```python
import functools

import jax
import jax.numpy as jnp
from jax import lax
from jax.experimental import pallas as pl
from jax.experimental.pallas import tpu as pltpu
from jax.sharding import PartitionSpec as P

CH = 64
DEPTH = 8
TAPS = 27
LANES = DEPTH * CH
PADDED = LANES + 2 * CH
PAIR = 2 * CH
PATCH = 4 * CH
KTOTAL = 3 * 16 * CH
MESH = pl.DeviceIdType.MESH
SENT_AFTER = 0
F32 = jnp.float32
BF16 = jnp.bfloat16

root_half = 0.7071067811865476
inv_root_two_pi = 0.3989422804014327


def round_up(value, multiple):
    return -(-value // multiple) * multiple


def kernel(
    sizes,
    x_hbm,
    g_hbm,
    k1_hbm,
    k2_hbm,
    gi_ref,
    fin_ref,
    xl,
    gl,
    kraw,
    kd,
    w1,
    w2,
    w3,
    esend,
    erecv,
    rowbuf,
    shifted,
    gpl,
    held,
    turned,
    sums,
    piece,
    got,
    total,
    window,
    wgot,
    local_sem,
    halo_send,
    halo_recv,
    core_send,
    core_recv,
    last_send,
    last_recv,
):
    n_ha, n_wa, rows, cols = sizes
    ha = lax.axis_index("ha")
    wa = lax.axis_index("wa")
    pairs = rows // 2
    rows_first = (TAPS * CH) // (2 * n_ha)
    exact = (TAPS * CH * CH) // (n_ha * n_wa)

    def wrap(value, size):
        value = jnp.where(value >= size, value - size, value)
        return jnp.where(value < 0, value + size, value)

    def ha_at(step):
        return wrap(ha + step, n_ha)

    def wa_at(step):
        return wrap(wa + step, n_wa)

    n_z = n_ha // 4
    core = lax.rem(ha, 2)
    upper = lax.rem(lax.div(ha, 2), 2)
    z_here = lax.div(ha, 4)
    other_core = ha + 1 - 2 * core

    barrier = pltpu.get_barrier_semaphore()
    peers = [(ha_at(a), wa) for a in (-1, 1)]
    peers += [(ha, wa_at(d)) for d in (-1, 1)[: n_wa - 1]]
    peers += [(ha_at(a), wa_at(b)) for a in (-1, 1) for b in (-1, 1)]
    chips = []
    for dz in range(n_z):
        for du in range(2):
            for dw in range(n_wa):
                if dz + du + dw:
                    to_z = wrap(z_here + dz, n_z)
                    to_u = upper if du == 0 else 1 - upper
                    chips.append(((to_z, to_u, wa_at(dw)), (to_z * 4 + to_u * 2 + core, wa_at(dw))))
                    if dz + du or 1 < dw < n_wa - 1:
                        peers.append(chips[-1][1])
    loads = [
        pltpu.make_async_copy(x_hbm, xl, local_sem.at[2]),
        pltpu.make_async_copy(g_hbm, gl, local_sem.at[3]),
        pltpu.make_async_copy(k1_hbm, kraw.at[0], local_sem.at[0]),
        pltpu.make_async_copy(k2_hbm, kraw.at[1], local_sem.at[1]),
    ]
    for peer in peers[:8]:
        pl.semaphore_signal(barrier, inc=1, device_id=peer, device_id_type=MESH)
    for load in loads:
        load.start()
    for peer in peers[8:]:
        pl.semaphore_signal(barrier, inc=1, device_id=peer, device_id_type=MESH)

    sent = []

    def edges(field_refs, side):
        start, pick = (0, 0) if side == 0 else (cols - 16, 15)
        ids = lax.broadcasted_iota(jnp.int32, (16, LANES), 0)
        value = jnp.zeros((16, LANES), F32)
        for f, ref in enumerate(field_refs):
            for h in range(rows):
                block = ref[h, start : start + 16, :].astype(F32)
                cell = jnp.broadcast_to(block[pick : pick + 1], (16, LANES))
                value = jnp.where(ids == f * 8 + h, cell, value)
        return value.astype(BF16)

    def exchange(phase, field_refs):
        rows_of = []
        for f, ref in enumerate(field_refs):
            slot = phase * 2 + f
            group = []
            for side, row, step in ((0, rows - 1, 1), (1, 0, -1)):
                group.append(
                    pltpu.make_async_remote_copy(
                        src_ref=ref.at[row],
                        dst_ref=rowbuf.at[slot, side],
                        send_sem=halo_send.at[phase, f * 2 + side],
                        recv_sem=halo_recv.at[phase, f * 2 + side],
                        device_id=(ha_at(step), wa),
                        device_id_type=MESH,
                    )
                )
            rows_of.append(group)
        corners = []
        for side, wa_step in ((0, -1), (1, 1)):
            for dh in (-1, 0, 1):
                slot = (1 - side) * 3 + 1 - dh
                corners.append(
                    pltpu.make_async_remote_copy(
                        src_ref=esend.at[phase, side],
                        dst_ref=erecv.at[phase, slot],
                        send_sem=halo_send.at[phase, 4 + slot],
                        recv_sem=halo_recv.at[phase, 4 + slot],
                        device_id=(ha_at(dh), wa_at(wa_step)),
                        device_id_type=MESH,
                    )
                )
        beside = [corners[1], corners[4]]
        corners = [corners[i] for i in (0, 2, 3, 5)]
        for group in [beside, rows_of[0], corners] + rows_of[1:]:
            for copy in group:
                copy.start()
            sent.extend(group)
        return beside, corners, rows_of

    def widen(value):
        zeros = jnp.zeros((value.shape[0], PADDED - LANES), F32)
        return pltpu.roll(jnp.concatenate([value, zeros], axis=1), CH, 1)

    low_ok = ha > 0
    high_ok = ha < n_ha - 1
    left_ok = wa > 0
    right_ok = wa < n_wa - 1
    cell_ids = lax.broadcasted_iota(jnp.int32, (cols, PADDED), 0)
    tile_ids = lax.broadcasted_iota(jnp.int32, (16, PADDED), 0)

    def own_rows(ref, dst):
        for h in range(rows):
            value = widen(ref[h].astype(F32))
            shifted[dst, 0, h + 1] = pltpu.roll(value, 1, 0).astype(BF16)
            shifted[dst, 1, h + 1] = value.astype(BF16)
            shifted[dst, 2, h + 1] = pltpu.roll(value, cols - 1, 0).astype(BF16)

    def halo_cells(phase, side, r):
        ok = (left_ok, right_ok)[side]
        if r != 1:
            ok = jnp.logical_and(ok, (low_ok, None, high_ok)[r])
        return jnp.where(ok, widen(erecv[phase, side * 3 + r].astype(F32)), 0.0)

    def finish_own(phase, f, dst):
        sides = [halo_cells(phase, side, 1) for side in range(2)]
        for h in range(rows):
            left = sides[0][f * 8 + h : f * 8 + h + 1]
            right = sides[1][f * 8 + h : f * 8 + h + 1]
            tile = shifted[dst, 0, h + 1, 0:16, :].astype(F32)
            tile = jnp.where(tile_ids == 0, jnp.broadcast_to(left, (16, PADDED)), tile)
            shifted[dst, 0, h + 1, 0:16, :] = tile.astype(BF16)
            tile = shifted[dst, 2, h + 1, cols - 16 : cols, :].astype(F32)
            tile = jnp.where(tile_ids == 15, jnp.broadcast_to(right, (16, PADDED)), tile)
            shifted[dst, 2, h + 1, cols - 16 : cols, :] = tile.astype(BF16)

    def outer_rows(phase, f, dst):
        slot = phase * 2 + f
        for e, side, ok, r, h in ((0, 0, low_ok, 0, rows - 1), (rows + 1, 1, high_ok, 2, 0)):
            value = widen(jnp.where(ok, rowbuf[slot, side].astype(F32), 0.0))
            left = halo_cells(phase, 0, r)[f * 8 + h : f * 8 + h + 1]
            right = halo_cells(phase, 1, r)[f * 8 + h : f * 8 + h + 1]
            before = jnp.where(
                cell_ids == 0,
                jnp.broadcast_to(left, (cols, PADDED)),
                pltpu.roll(value, 1, 0),
            )
            after = jnp.where(
                cell_ids == cols - 1,
                jnp.broadcast_to(right, (cols, PADDED)),
                pltpu.roll(value, cols - 1, 0),
            )
            shifted[dst, 0, e] = before.astype(BF16)
            shifted[dst, 1, e] = value.astype(BF16)
            shifted[dst, 2, e] = after.astype(BF16)

    lane_low = lax.broadcasted_iota(jnp.int32, (CH, PAIR), 1) < CH
    zero_block = jnp.zeros((CH, PAIR), BF16)

    def double():
        @pl.loop(0, 9)
        def _(ab):
            for c in range(3):
                for which in range(2):
                    block = kraw[which, ab * 3 + c]
                    kd[which, ab * 3 + c] = jnp.concatenate([block, block], axis=1)

    def tap_block(which, index, c):
        return kd[which, index(c)] if 0 <= c <= 2 else zero_block

    def build_rows(which, dst):
        @pl.loop(0, 3)
        def _(b):
            base = b * 16 * CH
            for di in range(4):
                for a in range(4):
                    if a < 3:
                        index = lambda c: 9 * a + 3 * b + c
                        tile = jnp.where(
                            lane_low,
                            tap_block(which, index, di),
                            tap_block(which, index, di - 1),
                        )
                    else:
                        tile = zero_block
                    here = pl.multiple_of(base + (a * 4 + di) * CH, CH)
                    dst[pl.ds(here, CH), 0:PAIR] = tile
                    here = pl.multiple_of(base + ((a + 1) % 4 * 4 + di) * CH, CH)
                    dst[pl.ds(here, CH), PAIR : 2 * PAIR] = tile

    def build_turned(which, dst):
        @pl.loop(0, 3)
        def _(b):
            base = b * 16 * CH
            for dd in range(2):
                for m in range(2):
                    for a in range(4):
                        if a < 3:
                            index = lambda c: TAPS - 1 - (9 * a + 3 * b + c)
                            tile = jnp.where(
                                lane_low,
                                tap_block(which, index, 2 * m - dd),
                                tap_block(which, index, 2 * m + 1 - dd),
                            )
                        else:
                            tile = zero_block
                        here = pl.multiple_of(base + (a * 4 + 2 * m) * CH, 128)
                        dst[dd * CH : (dd + 1) * CH, pl.ds(here, PAIR)] = tile
                        here = pl.multiple_of(base + ((a + 1) % 4 * 4 + 2 * m) * CH, 128)
                        dst[PAIR + dd * CH : PAIR + (dd + 1) * CH, pl.ds(here, PAIR)] = tile

    loads[0].wait()
    loads[1].wait()
    for side in range(2):
        esend[0, side] = edges((xl, gl), side)
    pl.semaphore_wait(barrier, len(peers))
    beside, corners, row_copies = exchange(0, (xl, gl))

    loads[2].wait()
    loads[3].wait()
    double()
    build_rows(0, w1)
    build_turned(1, w2)
    build_turned(0, w3)
    own_rows(xl, 0)
    own_rows(gl, 1)

    for copy in beside:
        copy.wait_recv()
    finish_own(0, 0, 0)
    finish_own(0, 1, 1)

    def patches(src, b, i, hp):
        return jnp.concatenate(
            [
                shifted[src, b, 2 * hp + i, :, dp * PAIR : dp * PAIR + PATCH]
                for dp in range(DEPTH // 2)
            ],
            axis=0,
        )

    def inner(hp):
        return [i for i in range(4) if 0 < 2 * hp + i < rows + 1]

    def outer(hp):
        return [i for i in range(4) if i not in inner(hp)]

    def conv(src, hp, weights, flipped, window_rows):
        spots = [(b, i) for b in range(3) for i in window_rows]
        left = jnp.concatenate([patches(src, b, i, hp) for b, i in spots], axis=1)
        parts = [slice((b * 4 + i) * PATCH, (b * 4 + i + 1) * PATCH) for b, i in spots]
        if flipped:
            right = jnp.concatenate([weights[:, part] for part in parts], axis=1)
            dims = (((1,), (1,)), ((), ()))
        else:
            right = jnp.concatenate([weights[part, :] for part in parts], axis=0)
            dims = (((1,), (0,)), ((), ()))
        return lax.dot_general(left, right, dims, preferred_element_type=F32)

    def spread(dst, hp, value):
        for hh in range(2):
            for dp in range(DEPTH // 2):
                dst[2 * hp + hh, :, dp * PAIR : (dp + 1) * PAIR] = value[
                    dp * cols : (dp + 1) * cols, hh * PAIR : (hh + 1) * PAIR
                ]

    block = cols * (DEPTH // 2)
    for hp in range(pairs):
        held[0, hp] = conv(0, hp, w1, False, inner(hp))
        held[1, hp] = conv(1, hp, w2, True, inner(hp))
    for copy in row_copies[0] + corners:
        copy.wait_recv()
    outer_rows(0, 0, 0)
    for hp in range(pairs):
        pre = held[0, hp] + conv(0, hp, w1, False, outer(hp))
        phi = 0.5 * (1.0 + lax.erf(pre * root_half))
        turned[1, :, hp * block : (hp + 1) * block] = (pre * phi).astype(BF16).T
        held[0, hp] = phi + pre * inv_root_two_pi * jnp.exp(-0.5 * pre * pre)
    for copy in row_copies[1]:
        copy.wait_recv()
    outer_rows(0, 1, 1)
    for hp in range(pairs):
        grad_active = held[1, hp] + conv(1, hp, w2, True, outer(hp))
        grad_pre = (grad_active * held[0, hp]).astype(BF16)
        spread(gpl, hp, grad_pre)
        turned[0, :, hp * block : (hp + 1) * block] = grad_pre.T

    half = lax.broadcasted_iota(jnp.int32, (CH, PAIR), 1) < CH

    def gradients(src, b):
        blocks = []
        for i in range(4):
            right = jnp.concatenate([patches(src, b, i, hp) for hp in range(pairs)], axis=0)
            blocks.append(
                lax.dot_general(
                    turned[src],
                    right,
                    (((1,), (0,)), ((), ())),
                    preferred_element_type=F32,
                )
            )
        for a in range(3):
            low, high = blocks[a], blocks[a + 1]
            even = low[0:CH] + high[PAIR : PAIR + CH]
            odd = low[CH:PAIR] + high[PAIR + CH : 2 * PAIR]
            yield a, even[:, :PAIR], even[:, PAIR:], odd[:, :PAIR], odd[:, PAIR:]

    def send_to_core(which):
        for j in range(n_ha):
            first = sums[which, pl.ds(2 * j * rows_first, rows_first, stride=2), :]
            second = sums[which, pl.ds(2 * j * rows_first + 1, rows_first, stride=2), :]
            value = jnp.where(
                lax.broadcasted_iota(jnp.int32, (rows_first, PAIR), 1) < CH,
                first,
                pltpu.roll(second, CH, 1),
            )
            piece[which, j % 2, j // 2, 0:rows_first, :] = value.astype(BF16)
        copy = pltpu.make_async_remote_copy(
            src_ref=piece.at[which, 1 - core],
            dst_ref=got.at[which],
            send_sem=core_send.at[which],
            recv_sem=core_recv.at[which],
            device_id=(other_core, wa),
            device_id_type=MESH,
        )
        copy.start()
        sent.append(copy)
        return copy

    starts = [(k * rows_first) // n_wa for k in range(n_wa)]
    span = window.shape[4]

    def send_to_chips(which, arrival):
        arrival.wait_recv()
        for t in range(n_ha // 2):
            total[t] = piece[which, core, t].astype(F32) + got[which, t].astype(F32)
        for t in range(n_ha // 2):
            for k in range(n_wa):
                value = total[t, starts[k] : starts[k] + span, :]
                window[which, t // 2, t % 2, k] = value.astype(BF16)
        copies = []
        for i, ((to_z, to_u, to_w), peer) in enumerate(chips):
            copies.append(
                pltpu.make_async_remote_copy(
                    src_ref=window.at[which, to_z, to_u, to_w],
                    dst_ref=wgot.at[which, i],
                    send_sem=last_send.at[which, i],
                    recv_sem=last_recv.at[which, i],
                    device_id=peer,
                    device_id_type=MESH,
                )
            )
        for copy in copies:
            copy.start()
        sent.extend(copies)
        return copies

    for b in range(3):
        for a, even0, even1, odd0, odd1 in gradients(1, b):
            turn = pltpu.roll(odd1, CH, 1)
            values = (even0 + pltpu.roll(odd0, CH, 1), odd1 + pltpu.roll(even0, CH, 1), even1 + turn)
            for c in range(3):
                start = (TAPS - 1 - (9 * a + 3 * b + c)) * CH
                sums[1, start : start + CH, :] = values[c]
        if b == SENT_AFTER:
            for side in range(2):
                esend[1, side] = edges((gpl,), side)
            beside, corners, row_copies = exchange(1, (gpl,))
    arrivals = [None, send_to_core(1)]
    lasts = [None, None]
    for b in range(3):
        for a, even0, even1, odd0, odd1 in gradients(0, b):
            turn = pltpu.roll(odd1, CH, 1)
            both = even0 + jnp.where(half, pltpu.roll(odd0, CH, 1), turn)
            start = (9 * a + 3 * b) * CH
            sums[0, start : start + 2 * CH, 0:CH] = both.T
            sums[0, start + 2 * CH : start + 3 * CH, 0:CH] = (even1 + turn).T[0:CH]
    arrivals[0] = send_to_core(0)

    lasts[1] = send_to_chips(1, arrivals[1])
    lasts[0] = send_to_chips(0, arrivals[0])
    own_rows(gpl, 2)
    for copy in beside + corners + row_copies[0]:
        copy.wait_recv()
    finish_own(1, 0, 2)
    outer_rows(1, 0, 2)
    for hp in range(pairs):
        spread(gi_ref, hp, conv(2, hp, w3, True, range(4)).astype(BF16))

    for which in (1, 0):
        value = window[which, z_here, upper, wa].astype(F32)
        for copy in lasts[which]:
            copy.wait_recv()
        fin_ref[which] = value + jnp.sum(wgot[which].astype(F32), axis=0)
    for copy in sent:
        copy.wait_send()


def finish(sizes, gi_ref, fin_ref, gi_hbm, one_ref, two_ref, sem):
    n_ha, n_wa, rows, cols = sizes
    wa = lax.axis_index("wa")
    exact = (TAPS * CH * CH) // (n_ha * n_wa)
    store = pltpu.make_async_copy(gi_ref, gi_hbm, sem)
    store.start()
    offset = lax.rem(wa * exact, 128)
    count = -(-exact // 128)
    lanes = lax.broadcasted_iota(jnp.int32, (count, 128), 1)
    for which, out in ((0, one_ref), (1, two_ref)):
        value = pltpu.roll(fin_ref[which], 128 - offset, 1)
        value = jnp.where(lanes < 128 - offset, value[0:count], value[1 : count + 1])
        for r in range(count):
            width = min(128, exact - r * 128)
            out[pl.ds(r * 128, width)] = value[r, 0:width]
    store.wait()


def shards(sizes, inputs, grad_out, kernel_one, kernel_two):
    n_ha, n_wa, rows, cols = sizes
    rows_first = (TAPS * CH) // (2 * n_ha)
    exact = (TAPS * CH * CH) // (n_ha * n_wa)
    out_rows = -(-exact // 128)
    span = round_up(out_rows + 1, 8)
    first_pad = round_up(max(rows_first, (n_wa - 1) * rows_first // n_wa + span), 8)
    any_spec = pl.BlockSpec(memory_space=pl.ANY)
    vmem_spec = pl.BlockSpec(memory_space=pltpu.VMEM)
    dma = pltpu.SemaphoreType.DMA
    grad_inputs, fin = pl.pallas_call(
        functools.partial(kernel, sizes),
        out_shape=(
            pltpu.VMEM((rows, cols, LANES), BF16),
            pltpu.VMEM((2, span, 128), F32),
        ),
        in_specs=[pl.BlockSpec(memory_space=pltpu.HBM)] * 4,
        out_specs=(vmem_spec, vmem_spec),
        scratch_shapes=[
            pltpu.VMEM((rows, cols, LANES), BF16),
            pltpu.VMEM((rows, cols, LANES), BF16),
            pltpu.VMEM((2, TAPS, CH, CH), BF16),
            pltpu.VMEM((2, TAPS, CH, PAIR), BF16),
            pltpu.VMEM((KTOTAL, PATCH), BF16),
            pltpu.VMEM((PATCH, KTOTAL), BF16),
            pltpu.VMEM((PATCH, KTOTAL), BF16),
            pltpu.VMEM((2, 2, 16, LANES), BF16),
            pltpu.VMEM((2, 6, 16, LANES), BF16),
            pltpu.VMEM((3, 2, cols, LANES), BF16),
            pltpu.VMEM((3, 3, rows + 2, cols, PADDED), BF16),
            pltpu.VMEM((rows, cols, LANES), BF16),
            pltpu.VMEM((2, rows // 2, cols * DEPTH // 2, PATCH), F32),
            pltpu.VMEM((2, PATCH, rows * cols * 2), BF16),
            pltpu.VMEM((2, TAPS * CH, PAIR), F32),
            pltpu.VMEM((2, 2, n_ha // 2, first_pad, 128), BF16),
            pltpu.VMEM((2, n_ha // 2, first_pad, 128), BF16),
            pltpu.VMEM((n_ha // 2, first_pad, 128), F32),
            pltpu.VMEM((2, n_ha // 4, 2, n_wa, span, 128), BF16),
            pltpu.VMEM((2, n_ha // 2 * n_wa - 1, span, 128), BF16),
            dma((4,)),
            dma((2, 10)),
            dma((2, 10)),
            dma((2,)),
            dma((2,)),
            dma((2, n_ha // 2 * n_wa - 1)),
            dma((2, n_ha // 2 * n_wa - 1)),
        ],
        compiler_params=pltpu.CompilerParams(
            collective_id=0, has_side_effects=True, vmem_limit_bytes=65024 * 1024
        ),
    )(inputs, grad_out, kernel_one, kernel_two)
    return pl.pallas_call(
        functools.partial(finish, sizes),
        out_shape=(
            jax.ShapeDtypeStruct((rows, cols, LANES), BF16),
            jax.ShapeDtypeStruct((exact,), F32),
            jax.ShapeDtypeStruct((exact,), F32),
        ),
        in_specs=[vmem_spec, vmem_spec],
        out_specs=(any_spec, vmem_spec, vmem_spec),
        scratch_shapes=[dma],
        compiler_params=pltpu.CompilerParams(vmem_limit_bytes=8 * 1024 * 1024),
    )(grad_inputs, fin)


def solution(mesh):
    n_ha, n_wa = mesh.shape["ha"], mesh.shape["wa"]

    def step(inputs, grad_out, kernel_one, kernel_two):
        rows, cols, _ = inputs.shape
        return shards((n_ha, n_wa, rows, cols), inputs, grad_out, kernel_one, kernel_two)

    return jax.shard_map(
        step,
        mesh=mesh,
        in_specs=(P("ha", "wa", None), P("ha", "wa", None), P(), P()),
        out_specs=(P("ha", "wa", None), P(("ha", "wa")), P(("ha", "wa"))),
        check_vma=False,
    )
```

```python
import functools

import jax
import jax.numpy as jnp
from jax import lax
from jax.experimental import pallas as pl
from jax.experimental.pallas import tpu as pltpu
from jax.sharding import PartitionSpec as P

CH = 64
DEPTH = 8
TAPS = 27
LANES = DEPTH * CH
PADDED = LANES + 2 * CH
PAIR = 2 * CH
PATCH = 4 * CH
KTOTAL = 3 * 16 * CH
MESH = pl.DeviceIdType.MESH
SENT_AFTER = 0
F32 = jnp.float32
BF16 = jnp.bfloat16

root_half = 0.7071067811865476
inv_root_two_pi = 0.3989422804014327


def round_up(value, multiple):
    return -(-value // multiple) * multiple


def kernel(
    sizes,
    x_hbm,
    g_hbm,
    k1_hbm,
    k2_hbm,
    gi_ref,
    fin_ref,
    xl,
    gl,
    kraw,
    kd,
    w1,
    w2,
    w3,
    esend,
    erecv,
    rowbuf,
    shifted,
    gpl,
    held,
    turned,
    sums,
    piece,
    got,
    total,
    window,
    wgot,
    local_sem,
    halo_send,
    halo_recv,
    core_send,
    core_recv,
    last_send,
    last_recv,
):
    n_ha, n_wa, rows, cols = sizes
    ha = lax.axis_index("ha")
    wa = lax.axis_index("wa")
    pairs = rows // 2
    rows_first = (TAPS * CH) // (2 * n_ha)
    exact = (TAPS * CH * CH) // (n_ha * n_wa)

    def wrap(value, size):
        value = jnp.where(value >= size, value - size, value)
        return jnp.where(value < 0, value + size, value)

    def ha_at(step):
        return wrap(ha + step, n_ha)

    def wa_at(step):
        return wrap(wa + step, n_wa)

    n_z = n_ha // 4
    core = lax.rem(ha, 2)
    upper = lax.rem(lax.div(ha, 2), 2)
    z_here = lax.div(ha, 4)
    other_core = ha + 1 - 2 * core

    barrier = pltpu.get_barrier_semaphore()
    peers = [(ha_at(a), wa) for a in (-1, 1)]
    peers += [(ha, wa_at(d)) for d in (-1, 1)[: n_wa - 1]]
    peers += [(ha_at(a), wa_at(b)) for a in (-1, 1) for b in (-1, 1)]
    chips = []
    for dz in range(n_z):
        for du in range(2):
            for dw in range(n_wa):
                if dz + du + dw:
                    to_z = wrap(z_here + dz, n_z)
                    to_u = upper if du == 0 else 1 - upper
                    chips.append(((to_z, to_u, wa_at(dw)), (to_z * 4 + to_u * 2 + core, wa_at(dw))))
                    if dz + du or 1 < dw < n_wa - 1:
                        peers.append(chips[-1][1])
    loads = [
        pltpu.make_async_copy(x_hbm, xl, local_sem.at[2]),
        pltpu.make_async_copy(g_hbm, gl, local_sem.at[3]),
        pltpu.make_async_copy(k1_hbm, kraw.at[0], local_sem.at[0]),
        pltpu.make_async_copy(k2_hbm, kraw.at[1], local_sem.at[1]),
    ]
    for peer in peers[:8]:
        pl.semaphore_signal(barrier, inc=1, device_id=peer, device_id_type=MESH)
    for load in loads:
        load.start()
    for peer in peers[8:]:
        pl.semaphore_signal(barrier, inc=1, device_id=peer, device_id_type=MESH)

    sent = []

    def edges(field_refs, side):
        start, pick = (0, 0) if side == 0 else (cols - 16, 15)
        ids = lax.broadcasted_iota(jnp.int32, (16, LANES), 0)
        value = jnp.zeros((16, LANES), F32)
        for f, ref in enumerate(field_refs):
            for h in range(rows):
                block = ref[h, start : start + 16, :].astype(F32)
                cell = jnp.broadcast_to(block[pick : pick + 1], (16, LANES))
                value = jnp.where(ids == f * 8 + h, cell, value)
        return value.astype(BF16)

    def exchange(phase, field_refs):
        rows_of = []
        for f, ref in enumerate(field_refs):
            slot = phase * 2 + f
            group = []
            for side, row, step in ((0, rows - 1, 1), (1, 0, -1)):
                group.append(
                    pltpu.make_async_remote_copy(
                        src_ref=ref.at[row],
                        dst_ref=rowbuf.at[slot, side],
                        send_sem=halo_send.at[phase, f * 2 + side],
                        recv_sem=halo_recv.at[phase, f * 2 + side],
                        device_id=(ha_at(step), wa),
                        device_id_type=MESH,
                    )
                )
            rows_of.append(group)
        corners = []
        for side, wa_step in ((0, -1), (1, 1)):
            for dh in (-1, 0, 1):
                slot = (1 - side) * 3 + 1 - dh
                corners.append(
                    pltpu.make_async_remote_copy(
                        src_ref=esend.at[phase, side],
                        dst_ref=erecv.at[phase, slot],
                        send_sem=halo_send.at[phase, 4 + slot],
                        recv_sem=halo_recv.at[phase, 4 + slot],
                        device_id=(ha_at(dh), wa_at(wa_step)),
                        device_id_type=MESH,
                    )
                )
        beside = [corners[1], corners[4]]
        corners = [corners[i] for i in (0, 2, 3, 5)]
        for group in [beside, rows_of[0], corners] + rows_of[1:]:
            for copy in group:
                copy.start()
            sent.extend(group)
        return beside, corners, rows_of

    def widen(value):
        zeros = jnp.zeros((value.shape[0], PADDED - LANES), F32)
        return pltpu.roll(jnp.concatenate([value, zeros], axis=1), CH, 1)

    low_ok = ha > 0
    high_ok = ha < n_ha - 1
    left_ok = wa > 0
    right_ok = wa < n_wa - 1
    cell_ids = lax.broadcasted_iota(jnp.int32, (cols, PADDED), 0)
    tile_ids = lax.broadcasted_iota(jnp.int32, (16, PADDED), 0)

    def own_rows(ref, dst):
        for h in range(rows):
            value = widen(ref[h].astype(F32))
            shifted[dst, 0, h + 1] = pltpu.roll(value, 1, 0).astype(BF16)
            shifted[dst, 1, h + 1] = value.astype(BF16)
            shifted[dst, 2, h + 1] = pltpu.roll(value, cols - 1, 0).astype(BF16)

    def halo_cells(phase, side, r):
        ok = (left_ok, right_ok)[side]
        if r != 1:
            ok = jnp.logical_and(ok, (low_ok, None, high_ok)[r])
        return jnp.where(ok, widen(erecv[phase, side * 3 + r].astype(F32)), 0.0)

    def finish_own(phase, f, dst):
        sides = [halo_cells(phase, side, 1) for side in range(2)]
        for h in range(rows):
            left = sides[0][f * 8 + h : f * 8 + h + 1]
            right = sides[1][f * 8 + h : f * 8 + h + 1]
            tile = shifted[dst, 0, h + 1, 0:16, :].astype(F32)
            tile = jnp.where(tile_ids == 0, jnp.broadcast_to(left, (16, PADDED)), tile)
            shifted[dst, 0, h + 1, 0:16, :] = tile.astype(BF16)
            tile = shifted[dst, 2, h + 1, cols - 16 : cols, :].astype(F32)
            tile = jnp.where(tile_ids == 15, jnp.broadcast_to(right, (16, PADDED)), tile)
            shifted[dst, 2, h + 1, cols - 16 : cols, :] = tile.astype(BF16)

    def outer_rows(phase, f, dst):
        slot = phase * 2 + f
        for e, side, ok, r, h in ((0, 0, low_ok, 0, rows - 1), (rows + 1, 1, high_ok, 2, 0)):
            value = widen(jnp.where(ok, rowbuf[slot, side].astype(F32), 0.0))
            left = halo_cells(phase, 0, r)[f * 8 + h : f * 8 + h + 1]
            right = halo_cells(phase, 1, r)[f * 8 + h : f * 8 + h + 1]
            before = jnp.where(
                cell_ids == 0,
                jnp.broadcast_to(left, (cols, PADDED)),
                pltpu.roll(value, 1, 0),
            )
            after = jnp.where(
                cell_ids == cols - 1,
                jnp.broadcast_to(right, (cols, PADDED)),
                pltpu.roll(value, cols - 1, 0),
            )
            shifted[dst, 0, e] = before.astype(BF16)
            shifted[dst, 1, e] = value.astype(BF16)
            shifted[dst, 2, e] = after.astype(BF16)

    lane_low = lax.broadcasted_iota(jnp.int32, (CH, PAIR), 1) < CH
    zero_block = jnp.zeros((CH, PAIR), BF16)

    def double():
        @pl.loop(0, 9)
        def _(ab):
            for c in range(3):
                for which in range(2):
                    block = kraw[which, ab * 3 + c]
                    kd[which, ab * 3 + c] = jnp.concatenate([block, block], axis=1)

    def tap_block(which, index, c):
        return kd[which, index(c)] if 0 <= c <= 2 else zero_block

    def build_rows(which, dst):
        @pl.loop(0, 3)
        def _(b):
            base = b * 16 * CH
            for di in range(4):
                for a in range(4):
                    if a < 3:
                        index = lambda c: 9 * a + 3 * b + c
                        tile = jnp.where(
                            lane_low,
                            tap_block(which, index, di),
                            tap_block(which, index, di - 1),
                        )
                    else:
                        tile = zero_block
                    here = pl.multiple_of(base + (a * 4 + di) * CH, CH)
                    dst[pl.ds(here, CH), 0:PAIR] = tile
                    here = pl.multiple_of(base + ((a + 1) % 4 * 4 + di) * CH, CH)
                    dst[pl.ds(here, CH), PAIR : 2 * PAIR] = tile

    def build_turned(which, dst):
        @pl.loop(0, 3)
        def _(b):
            base = b * 16 * CH
            for dd in range(2):
                for m in range(2):
                    for a in range(4):
                        if a < 3:
                            index = lambda c: TAPS - 1 - (9 * a + 3 * b + c)
                            tile = jnp.where(
                                lane_low,
                                tap_block(which, index, 2 * m - dd),
                                tap_block(which, index, 2 * m + 1 - dd),
                            )
                        else:
                            tile = zero_block
                        here = pl.multiple_of(base + (a * 4 + 2 * m) * CH, 128)
                        dst[dd * CH : (dd + 1) * CH, pl.ds(here, PAIR)] = tile
                        here = pl.multiple_of(base + ((a + 1) % 4 * 4 + 2 * m) * CH, 128)
                        dst[PAIR + dd * CH : PAIR + (dd + 1) * CH, pl.ds(here, PAIR)] = tile

    loads[0].wait()
    loads[1].wait()
    for side in range(2):
        esend[0, side] = edges((xl, gl), side)
    pl.semaphore_wait(barrier, len(peers))
    beside, corners, row_copies = exchange(0, (xl, gl))

    loads[2].wait()
    loads[3].wait()
    double()
    build_rows(0, w1)
    build_turned(1, w2)
    build_turned(0, w3)
    own_rows(xl, 0)
    own_rows(gl, 1)

    for copy in beside:
        copy.wait_recv()
    finish_own(0, 0, 0)
    finish_own(0, 1, 1)

    def patches(src, b, i, hp):
        return jnp.concatenate(
            [
                shifted[src, b, 2 * hp + i, :, dp * PAIR : dp * PAIR + PATCH]
                for dp in range(DEPTH // 2)
            ],
            axis=0,
        )

    def inner(hp):
        return [i for i in range(4) if 0 < 2 * hp + i < rows + 1]

    def outer(hp):
        return [i for i in range(4) if i not in inner(hp)]

    def conv(src, hp, weights, flipped, window_rows):
        spots = [(b, i) for b in range(3) for i in window_rows]
        left = jnp.concatenate([patches(src, b, i, hp) for b, i in spots], axis=1)
        parts = [slice((b * 4 + i) * PATCH, (b * 4 + i + 1) * PATCH) for b, i in spots]
        if flipped:
            right = jnp.concatenate([weights[:, part] for part in parts], axis=1)
            dims = (((1,), (1,)), ((), ()))
        else:
            right = jnp.concatenate([weights[part, :] for part in parts], axis=0)
            dims = (((1,), (0,)), ((), ()))
        return lax.dot_general(left, right, dims, preferred_element_type=F32)

    def spread(dst, hp, value):
        for hh in range(2):
            for dp in range(DEPTH // 2):
                dst[2 * hp + hh, :, dp * PAIR : (dp + 1) * PAIR] = value[
                    dp * cols : (dp + 1) * cols, hh * PAIR : (hh + 1) * PAIR
                ]

    block = cols * (DEPTH // 2)
    for hp in range(pairs):
        held[0, hp] = conv(0, hp, w1, False, inner(hp))
        held[1, hp] = conv(1, hp, w2, True, inner(hp))
    for copy in row_copies[0] + corners:
        copy.wait_recv()
    outer_rows(0, 0, 0)
    for hp in range(pairs):
        pre = held[0, hp] + conv(0, hp, w1, False, outer(hp))
        phi = 0.5 * (1.0 + lax.erf(pre * root_half))
        turned[1, :, hp * block : (hp + 1) * block] = (pre * phi).astype(BF16).T
        held[0, hp] = phi + pre * inv_root_two_pi * jnp.exp(-0.5 * pre * pre)
    for copy in row_copies[1]:
        copy.wait_recv()
    outer_rows(0, 1, 1)
    for hp in range(pairs):
        grad_active = held[1, hp] + conv(1, hp, w2, True, outer(hp))
        grad_pre = (grad_active * held[0, hp]).astype(BF16)
        spread(gpl, hp, grad_pre)
        turned[0, :, hp * block : (hp + 1) * block] = grad_pre.T

    half = lax.broadcasted_iota(jnp.int32, (CH, PAIR), 1) < CH

    def gradients(src, b):
        blocks = []
        for i in range(4):
            right = jnp.concatenate([patches(src, b, i, hp) for hp in range(pairs)], axis=0)
            blocks.append(
                lax.dot_general(
                    turned[src],
                    right,
                    (((1,), (0,)), ((), ())),
                    preferred_element_type=F32,
                )
            )
        for a in range(3):
            low, high = blocks[a], blocks[a + 1]
            even = low[0:CH] + high[PAIR : PAIR + CH]
            odd = low[CH:PAIR] + high[PAIR + CH : 2 * PAIR]
            yield a, even[:, :PAIR], even[:, PAIR:], odd[:, :PAIR], odd[:, PAIR:]

    def send_to_core(which):
        for j in range(n_ha):
            first = sums[which, pl.ds(2 * j * rows_first, rows_first, stride=2), :]
            second = sums[which, pl.ds(2 * j * rows_first + 1, rows_first, stride=2), :]
            value = jnp.where(
                lax.broadcasted_iota(jnp.int32, (rows_first, PAIR), 1) < CH,
                first,
                pltpu.roll(second, CH, 1),
            )
            piece[which, j % 2, j // 2, 0:rows_first, :] = value.astype(BF16)
        copy = pltpu.make_async_remote_copy(
            src_ref=piece.at[which, 1 - core],
            dst_ref=got.at[which],
            send_sem=core_send.at[which],
            recv_sem=core_recv.at[which],
            device_id=(other_core, wa),
            device_id_type=MESH,
        )
        copy.start()
        sent.append(copy)
        return copy

    starts = [(k * rows_first) // n_wa for k in range(n_wa)]
    span = window.shape[4]

    def merge_cores(which, arrival):
        arrival.wait_recv()
        for t in range(n_ha // 2):
            total[t] = piece[which, core, t].astype(F32) + got[which, t].astype(F32)
        for t in range(n_ha // 2):
            for k in range(n_wa):
                value = total[t, starts[k] : starts[k] + span, :]
                window[t // 2, t % 2, k, which] = value.astype(BF16)

    def send_to_chips():
        copies = []
        for i, ((to_z, to_u, to_w), peer) in enumerate(chips):
            copies.append(
                pltpu.make_async_remote_copy(
                    src_ref=window.at[to_z, to_u, to_w],
                    dst_ref=wgot.at[i],
                    send_sem=last_send.at[i],
                    recv_sem=last_recv.at[i],
                    device_id=peer,
                    device_id_type=MESH,
                )
            )
        for copy in copies:
            copy.start()
        sent.extend(copies)
        return copies

    for b in range(3):
        for a, even0, even1, odd0, odd1 in gradients(1, b):
            turn = pltpu.roll(odd1, CH, 1)
            values = (even0 + pltpu.roll(odd0, CH, 1), odd1 + pltpu.roll(even0, CH, 1), even1 + turn)
            for c in range(3):
                start = (TAPS - 1 - (9 * a + 3 * b + c)) * CH
                sums[1, start : start + CH, :] = values[c]
        if b == SENT_AFTER:
            for side in range(2):
                esend[1, side] = edges((gpl,), side)
            beside, corners, row_copies = exchange(1, (gpl,))
    arrivals = [None, send_to_core(1)]
    for b in range(3):
        for a, even0, even1, odd0, odd1 in gradients(0, b):
            turn = pltpu.roll(odd1, CH, 1)
            both = even0 + jnp.where(half, pltpu.roll(odd0, CH, 1), turn)
            start = (9 * a + 3 * b) * CH
            sums[0, start : start + 2 * CH, 0:CH] = both.T
            sums[0, start + 2 * CH : start + 3 * CH, 0:CH] = (even1 + turn).T[0:CH]
    arrivals[0] = send_to_core(0)

    merge_cores(1, arrivals[1])
    merge_cores(0, arrivals[0])
    lasts = send_to_chips()
    own_rows(gpl, 2)
    for copy in beside + corners + row_copies[0]:
        copy.wait_recv()
    finish_own(1, 0, 2)
    outer_rows(1, 0, 2)
    for hp in range(pairs):
        spread(gi_ref, hp, conv(2, hp, w3, True, range(4)).astype(BF16))

    value = window[z_here, upper, wa].astype(F32)
    for copy in lasts:
        copy.wait_recv()
    fin_ref[...] = value + jnp.sum(wgot[...].astype(F32), axis=0)
    for copy in sent:
        copy.wait_send()


def finish(sizes, gi_ref, fin_ref, gi_hbm, one_ref, two_ref, sem):
    n_ha, n_wa, rows, cols = sizes
    wa = lax.axis_index("wa")
    exact = (TAPS * CH * CH) // (n_ha * n_wa)
    store = pltpu.make_async_copy(gi_ref, gi_hbm, sem)
    store.start()
    offset = lax.rem(wa * exact, 128)
    count = -(-exact // 128)
    lanes = lax.broadcasted_iota(jnp.int32, (count, 128), 1)
    for which, out in ((0, one_ref), (1, two_ref)):
        value = pltpu.roll(fin_ref[which], 128 - offset, 1)
        value = jnp.where(lanes < 128 - offset, value[0:count], value[1 : count + 1])
        for r in range(count):
            width = min(128, exact - r * 128)
            out[pl.ds(r * 128, width)] = value[r, 0:width]
    store.wait()


def shards(sizes, inputs, grad_out, kernel_one, kernel_two):
    n_ha, n_wa, rows, cols = sizes
    rows_first = (TAPS * CH) // (2 * n_ha)
    exact = (TAPS * CH * CH) // (n_ha * n_wa)
    out_rows = -(-exact // 128)
    span = round_up(out_rows + 1, 8)
    first_pad = round_up(max(rows_first, (n_wa - 1) * rows_first // n_wa + span), 8)
    any_spec = pl.BlockSpec(memory_space=pl.ANY)
    vmem_spec = pl.BlockSpec(memory_space=pltpu.VMEM)
    dma = pltpu.SemaphoreType.DMA
    grad_inputs, fin = pl.pallas_call(
        functools.partial(kernel, sizes),
        out_shape=(
            pltpu.VMEM((rows, cols, LANES), BF16),
            pltpu.VMEM((2, span, 128), F32),
        ),
        in_specs=[pl.BlockSpec(memory_space=pltpu.HBM)] * 4,
        out_specs=(vmem_spec, vmem_spec),
        scratch_shapes=[
            pltpu.VMEM((rows, cols, LANES), BF16),
            pltpu.VMEM((rows, cols, LANES), BF16),
            pltpu.VMEM((2, TAPS, CH, CH), BF16),
            pltpu.VMEM((2, TAPS, CH, PAIR), BF16),
            pltpu.VMEM((KTOTAL, PATCH), BF16),
            pltpu.VMEM((PATCH, KTOTAL), BF16),
            pltpu.VMEM((PATCH, KTOTAL), BF16),
            pltpu.VMEM((2, 2, 16, LANES), BF16),
            pltpu.VMEM((2, 6, 16, LANES), BF16),
            pltpu.VMEM((3, 2, cols, LANES), BF16),
            pltpu.VMEM((3, 3, rows + 2, cols, PADDED), BF16),
            pltpu.VMEM((rows, cols, LANES), BF16),
            pltpu.VMEM((2, rows // 2, cols * DEPTH // 2, PATCH), F32),
            pltpu.VMEM((2, PATCH, rows * cols * 2), BF16),
            pltpu.VMEM((2, TAPS * CH, PAIR), F32),
            pltpu.VMEM((2, 2, n_ha // 2, first_pad, 128), BF16),
            pltpu.VMEM((2, n_ha // 2, first_pad, 128), BF16),
            pltpu.VMEM((n_ha // 2, first_pad, 128), F32),
            pltpu.VMEM((n_ha // 4, 2, n_wa, 2, span, 128), BF16),
            pltpu.VMEM((n_ha // 2 * n_wa - 1, 2, span, 128), BF16),
            dma((4,)),
            dma((2, 10)),
            dma((2, 10)),
            dma((2,)),
            dma((2,)),
            dma((n_ha // 2 * n_wa - 1,)),
            dma((n_ha // 2 * n_wa - 1,)),
        ],
        compiler_params=pltpu.CompilerParams(
            collective_id=0, has_side_effects=True, vmem_limit_bytes=65024 * 1024
        ),
    )(inputs, grad_out, kernel_one, kernel_two)
    return pl.pallas_call(
        functools.partial(finish, sizes),
        out_shape=(
            jax.ShapeDtypeStruct((rows, cols, LANES), BF16),
            jax.ShapeDtypeStruct((exact,), F32),
            jax.ShapeDtypeStruct((exact,), F32),
        ),
        in_specs=[vmem_spec, vmem_spec],
        out_specs=(any_spec, vmem_spec, vmem_spec),
        scratch_shapes=[dma],
        compiler_params=pltpu.CompilerParams(vmem_limit_bytes=8 * 1024 * 1024),
    )(grad_inputs, fin)


def solution(mesh):
    n_ha, n_wa = mesh.shape["ha"], mesh.shape["wa"]

    def step(inputs, grad_out, kernel_one, kernel_two):
        rows, cols, _ = inputs.shape
        return shards((n_ha, n_wa, rows, cols), inputs, grad_out, kernel_one, kernel_two)

    return jax.shard_map(
        step,
        mesh=mesh,
        in_specs=(P("ha", "wa", None), P("ha", "wa", None), P(), P()),
        out_specs=(P("ha", "wa", None), P(("ha", "wa")), P(("ha", "wa"))),
        check_vma=False,
    )
```

```python
import functools

import jax
import jax.numpy as jnp
from jax import lax
from jax.experimental import pallas as pl
from jax.experimental.pallas import tpu as pltpu
from jax.sharding import PartitionSpec as P

CH = 64
DEPTH = 8
TAPS = 27
LANES = DEPTH * CH
PADDED = LANES + 2 * CH
PAIR = 2 * CH
PATCH = 4 * CH
KTOTAL = 3 * 16 * CH
MESH = pl.DeviceIdType.MESH
SENT_AFTER = 2
F32 = jnp.float32
BF16 = jnp.bfloat16

root_half = 0.7071067811865476
inv_root_two_pi = 0.3989422804014327


def round_up(value, multiple):
    return -(-value // multiple) * multiple


def kernel(
    sizes,
    x_hbm,
    g_hbm,
    k1_hbm,
    k2_hbm,
    gi_ref,
    fin_ref,
    xl,
    gl,
    kraw,
    kd,
    w1,
    w2,
    w3,
    esend,
    erecv,
    rowbuf,
    shifted,
    gpl,
    held,
    turned,
    sums,
    piece,
    got,
    total,
    window,
    wgot,
    local_sem,
    halo_send,
    halo_recv,
    core_send,
    core_recv,
    last_send,
    last_recv,
):
    n_ha, n_wa, rows, cols = sizes
    ha = lax.axis_index("ha")
    wa = lax.axis_index("wa")
    pairs = rows // 2
    rows_first = (TAPS * CH) // (2 * n_ha)
    exact = (TAPS * CH * CH) // (n_ha * n_wa)

    def wrap(value, size):
        value = jnp.where(value >= size, value - size, value)
        return jnp.where(value < 0, value + size, value)

    def ha_at(step):
        return wrap(ha + step, n_ha)

    def wa_at(step):
        return wrap(wa + step, n_wa)

    n_z = n_ha // 4
    core = lax.rem(ha, 2)
    upper = lax.rem(lax.div(ha, 2), 2)
    z_here = lax.div(ha, 4)
    other_core = ha + 1 - 2 * core

    barrier = pltpu.get_barrier_semaphore()
    peers = [(ha_at(a), wa) for a in (-1, 1)]
    peers += [(ha, wa_at(d)) for d in (-1, 1)[: n_wa - 1]]
    peers += [(ha_at(a), wa_at(b)) for a in (-1, 1) for b in (-1, 1)]
    chips = []
    for dz in range(n_z):
        for du in range(2):
            for dw in range(n_wa):
                if dz + du + dw:
                    to_z = wrap(z_here + dz, n_z)
                    to_u = upper if du == 0 else 1 - upper
                    far = min(dz, n_z - dz) + 2 * du + min(dw, n_wa - dw)
                    peer = (to_z * 4 + to_u * 2 + core, wa_at(dw))
                    chips.append((-far, (to_z, to_u, wa_at(dw)), peer))
                    if dz + du or 1 < dw < n_wa - 1:
                        peers.append(peer)
    chips = [entry[1:] for entry in sorted(chips, key=lambda entry: entry[0])]
    loads = [
        pltpu.make_async_copy(x_hbm, xl, local_sem.at[2]),
        pltpu.make_async_copy(g_hbm, gl, local_sem.at[3]),
        pltpu.make_async_copy(k1_hbm, kraw.at[0], local_sem.at[0]),
        pltpu.make_async_copy(k2_hbm, kraw.at[1], local_sem.at[1]),
    ]
    for peer in peers[:8]:
        pl.semaphore_signal(barrier, inc=1, device_id=peer, device_id_type=MESH)
    for load in loads:
        load.start()
    for peer in peers[8:]:
        pl.semaphore_signal(barrier, inc=1, device_id=peer, device_id_type=MESH)

    sent = []

    def edges(field_refs, side):
        start, pick = (0, 0) if side == 0 else (cols - 16, 15)
        ids = lax.broadcasted_iota(jnp.int32, (16, LANES), 0)
        value = jnp.zeros((16, LANES), F32)
        for f, ref in enumerate(field_refs):
            for h in range(rows):
                block = ref[h, start : start + 16, :].astype(F32)
                cell = jnp.broadcast_to(block[pick : pick + 1], (16, LANES))
                value = jnp.where(ids == f * 8 + h, cell, value)
        return value.astype(BF16)

    def exchange(phase, field_refs):
        rows_of = []
        for f, ref in enumerate(field_refs):
            slot = phase * 2 + f
            group = []
            for side, row, step in ((0, rows - 1, 1), (1, 0, -1)):
                group.append(
                    pltpu.make_async_remote_copy(
                        src_ref=ref.at[row],
                        dst_ref=rowbuf.at[slot, side],
                        send_sem=halo_send.at[phase, f * 2 + side],
                        recv_sem=halo_recv.at[phase, f * 2 + side],
                        device_id=(ha_at(step), wa),
                        device_id_type=MESH,
                    )
                )
            rows_of.append(group)
        corners = []
        for side, wa_step in ((0, -1), (1, 1)):
            for dh in (-1, 0, 1):
                slot = (1 - side) * 3 + 1 - dh
                corners.append(
                    pltpu.make_async_remote_copy(
                        src_ref=esend.at[phase, side],
                        dst_ref=erecv.at[phase, slot],
                        send_sem=halo_send.at[phase, 4 + slot],
                        recv_sem=halo_recv.at[phase, 4 + slot],
                        device_id=(ha_at(dh), wa_at(wa_step)),
                        device_id_type=MESH,
                    )
                )
        beside = [corners[1], corners[4]]
        corners = [corners[i] for i in (0, 2, 3, 5)]
        for group in [beside, rows_of[0], corners] + rows_of[1:]:
            for copy in group:
                copy.start()
            sent.extend(group)
        return beside, corners, rows_of

    def widen(value):
        zeros = jnp.zeros((value.shape[0], PADDED - LANES), F32)
        return pltpu.roll(jnp.concatenate([value, zeros], axis=1), CH, 1)

    low_ok = ha > 0
    high_ok = ha < n_ha - 1
    left_ok = wa > 0
    right_ok = wa < n_wa - 1
    cell_ids = lax.broadcasted_iota(jnp.int32, (cols, PADDED), 0)
    tile_ids = lax.broadcasted_iota(jnp.int32, (16, PADDED), 0)

    def own_rows(ref, dst):
        for h in range(rows):
            value = widen(ref[h].astype(F32))
            shifted[dst, 0, h + 1] = pltpu.roll(value, 1, 0).astype(BF16)
            shifted[dst, 1, h + 1] = value.astype(BF16)
            shifted[dst, 2, h + 1] = pltpu.roll(value, cols - 1, 0).astype(BF16)

    def halo_cells(phase, side, r):
        ok = (left_ok, right_ok)[side]
        if r != 1:
            ok = jnp.logical_and(ok, (low_ok, None, high_ok)[r])
        return jnp.where(ok, widen(erecv[phase, side * 3 + r].astype(F32)), 0.0)

    def finish_own(phase, f, dst):
        sides = [halo_cells(phase, side, 1) for side in range(2)]
        for h in range(rows):
            left = sides[0][f * 8 + h : f * 8 + h + 1]
            right = sides[1][f * 8 + h : f * 8 + h + 1]
            tile = shifted[dst, 0, h + 1, 0:16, :].astype(F32)
            tile = jnp.where(tile_ids == 0, jnp.broadcast_to(left, (16, PADDED)), tile)
            shifted[dst, 0, h + 1, 0:16, :] = tile.astype(BF16)
            tile = shifted[dst, 2, h + 1, cols - 16 : cols, :].astype(F32)
            tile = jnp.where(tile_ids == 15, jnp.broadcast_to(right, (16, PADDED)), tile)
            shifted[dst, 2, h + 1, cols - 16 : cols, :] = tile.astype(BF16)

    def outer_rows(phase, f, dst):
        slot = phase * 2 + f
        for e, side, ok, r, h in ((0, 0, low_ok, 0, rows - 1), (rows + 1, 1, high_ok, 2, 0)):
            value = widen(jnp.where(ok, rowbuf[slot, side].astype(F32), 0.0))
            left = halo_cells(phase, 0, r)[f * 8 + h : f * 8 + h + 1]
            right = halo_cells(phase, 1, r)[f * 8 + h : f * 8 + h + 1]
            before = jnp.where(
                cell_ids == 0,
                jnp.broadcast_to(left, (cols, PADDED)),
                pltpu.roll(value, 1, 0),
            )
            after = jnp.where(
                cell_ids == cols - 1,
                jnp.broadcast_to(right, (cols, PADDED)),
                pltpu.roll(value, cols - 1, 0),
            )
            shifted[dst, 0, e] = before.astype(BF16)
            shifted[dst, 1, e] = value.astype(BF16)
            shifted[dst, 2, e] = after.astype(BF16)

    lane_low = lax.broadcasted_iota(jnp.int32, (CH, PAIR), 1) < CH
    zero_block = jnp.zeros((CH, PAIR), BF16)

    def double():
        @pl.loop(0, 9)
        def _(ab):
            for c in range(3):
                for which in range(2):
                    block = kraw[which, ab * 3 + c]
                    kd[which, ab * 3 + c] = jnp.concatenate([block, block], axis=1)

    def tap_block(which, index, c):
        return kd[which, index(c)] if 0 <= c <= 2 else zero_block

    def build_rows(which, dst):
        @pl.loop(0, 3)
        def _(b):
            base = b * 16 * CH
            for di in range(4):
                for a in range(4):
                    if a < 3:
                        index = lambda c: 9 * a + 3 * b + c
                        tile = jnp.where(
                            lane_low,
                            tap_block(which, index, di),
                            tap_block(which, index, di - 1),
                        )
                    else:
                        tile = zero_block
                    here = pl.multiple_of(base + (a * 4 + di) * CH, CH)
                    dst[pl.ds(here, CH), 0:PAIR] = tile
                    here = pl.multiple_of(base + ((a + 1) % 4 * 4 + di) * CH, CH)
                    dst[pl.ds(here, CH), PAIR : 2 * PAIR] = tile

    def build_turned(which, dst):
        @pl.loop(0, 3)
        def _(b):
            base = b * 16 * CH
            for dd in range(2):
                for m in range(2):
                    for a in range(4):
                        if a < 3:
                            index = lambda c: TAPS - 1 - (9 * a + 3 * b + c)
                            tile = jnp.where(
                                lane_low,
                                tap_block(which, index, 2 * m - dd),
                                tap_block(which, index, 2 * m + 1 - dd),
                            )
                        else:
                            tile = zero_block
                        here = pl.multiple_of(base + (a * 4 + 2 * m) * CH, 128)
                        dst[dd * CH : (dd + 1) * CH, pl.ds(here, PAIR)] = tile
                        here = pl.multiple_of(base + ((a + 1) % 4 * 4 + 2 * m) * CH, 128)
                        dst[PAIR + dd * CH : PAIR + (dd + 1) * CH, pl.ds(here, PAIR)] = tile

    loads[0].wait()
    loads[1].wait()
    for side in range(2):
        esend[0, side] = edges((xl, gl), side)
    pl.semaphore_wait(barrier, len(peers))
    beside, corners, row_copies = exchange(0, (xl, gl))

    loads[2].wait()
    loads[3].wait()
    double()
    build_rows(0, w1)
    build_turned(1, w2)
    build_turned(0, w3)
    own_rows(xl, 0)
    own_rows(gl, 1)

    for copy in beside:
        copy.wait_recv()
    finish_own(0, 0, 0)
    finish_own(0, 1, 1)

    def patches(src, b, i, hp):
        return jnp.concatenate(
            [
                shifted[src, b, 2 * hp + i, :, dp * PAIR : dp * PAIR + PATCH]
                for dp in range(DEPTH // 2)
            ],
            axis=0,
        )

    def inner(hp):
        return [i for i in range(4) if 0 < 2 * hp + i < rows + 1]

    def outer(hp):
        return [i for i in range(4) if i not in inner(hp)]

    def conv(src, hp, weights, flipped, window_rows):
        spots = [(b, i) for b in range(3) for i in window_rows]
        left = jnp.concatenate([patches(src, b, i, hp) for b, i in spots], axis=1)
        parts = [slice((b * 4 + i) * PATCH, (b * 4 + i + 1) * PATCH) for b, i in spots]
        if flipped:
            right = jnp.concatenate([weights[:, part] for part in parts], axis=1)
            dims = (((1,), (1,)), ((), ()))
        else:
            right = jnp.concatenate([weights[part, :] for part in parts], axis=0)
            dims = (((1,), (0,)), ((), ()))
        return lax.dot_general(left, right, dims, preferred_element_type=F32)

    def spread(dst, hp, value):
        for hh in range(2):
            for dp in range(DEPTH // 2):
                dst[2 * hp + hh, :, dp * PAIR : (dp + 1) * PAIR] = value[
                    dp * cols : (dp + 1) * cols, hh * PAIR : (hh + 1) * PAIR
                ]

    block = cols * (DEPTH // 2)
    for hp in range(pairs):
        held[0, hp] = conv(0, hp, w1, False, inner(hp))
        held[1, hp] = conv(1, hp, w2, True, inner(hp))
    for copy in row_copies[0] + corners:
        copy.wait_recv()
    outer_rows(0, 0, 0)
    for hp in range(pairs):
        pre = held[0, hp] + conv(0, hp, w1, False, outer(hp))
        phi = 0.5 * (1.0 + lax.erf(pre * root_half))
        turned[1, :, hp * block : (hp + 1) * block] = (pre * phi).astype(BF16).T
        held[0, hp] = phi + pre * inv_root_two_pi * jnp.exp(-0.5 * pre * pre)
    for copy in row_copies[1]:
        copy.wait_recv()
    outer_rows(0, 1, 1)
    for hp in range(pairs):
        grad_active = held[1, hp] + conv(1, hp, w2, True, outer(hp))
        grad_pre = (grad_active * held[0, hp]).astype(BF16)
        spread(gpl, hp, grad_pre)
        turned[0, :, hp * block : (hp + 1) * block] = grad_pre.T

    half = lax.broadcasted_iota(jnp.int32, (CH, PAIR), 1) < CH

    def gradients(src, b):
        blocks = []
        for i in range(4):
            right = jnp.concatenate([patches(src, b, i, hp) for hp in range(pairs)], axis=0)
            blocks.append(
                lax.dot_general(
                    turned[src],
                    right,
                    (((1,), (0,)), ((), ())),
                    preferred_element_type=F32,
                )
            )
        for a in range(3):
            low, high = blocks[a], blocks[a + 1]
            even = low[0:CH] + high[PAIR : PAIR + CH]
            odd = low[CH:PAIR] + high[PAIR + CH : 2 * PAIR]
            yield a, even[:, :PAIR], even[:, PAIR:], odd[:, :PAIR], odd[:, PAIR:]

    def send_to_core(which):
        for j in range(n_ha):
            first = sums[which, pl.ds(2 * j * rows_first, rows_first, stride=2), :]
            second = sums[which, pl.ds(2 * j * rows_first + 1, rows_first, stride=2), :]
            value = jnp.where(
                lax.broadcasted_iota(jnp.int32, (rows_first, PAIR), 1) < CH,
                first,
                pltpu.roll(second, CH, 1),
            )
            piece[which, j % 2, j // 2, 0:rows_first, :] = value.astype(BF16)
        copy = pltpu.make_async_remote_copy(
            src_ref=piece.at[which, 1 - core],
            dst_ref=got.at[which],
            send_sem=core_send.at[which],
            recv_sem=core_recv.at[which],
            device_id=(other_core, wa),
            device_id_type=MESH,
        )
        copy.start()
        sent.append(copy)
        return copy

    starts = [(k * rows_first) // n_wa for k in range(n_wa)]
    span = window.shape[4]

    def merge_cores(which, arrival):
        arrival.wait_recv()
        for t in range(n_ha // 2):
            total[t] = piece[which, core, t].astype(F32) + got[which, t].astype(F32)
        for t in range(n_ha // 2):
            for k in range(n_wa):
                value = total[t, starts[k] : starts[k] + span, :]
                window[t // 2, t % 2, k, which] = value.astype(BF16)

    def send_to_chips():
        copies = []
        for i, ((to_z, to_u, to_w), peer) in enumerate(chips):
            copies.append(
                pltpu.make_async_remote_copy(
                    src_ref=window.at[to_z, to_u, to_w],
                    dst_ref=wgot.at[i],
                    send_sem=last_send.at[i],
                    recv_sem=last_recv.at[i],
                    device_id=peer,
                    device_id_type=MESH,
                )
            )
        for copy in copies:
            copy.start()
        sent.extend(copies)
        return copies

    for b in range(3):
        for a, even0, even1, odd0, odd1 in gradients(1, b):
            turn = pltpu.roll(odd1, CH, 1)
            values = (even0 + pltpu.roll(odd0, CH, 1), odd1 + pltpu.roll(even0, CH, 1), even1 + turn)
            for c in range(3):
                start = (TAPS - 1 - (9 * a + 3 * b + c)) * CH
                sums[1, start : start + CH, :] = values[c]
        if b == SENT_AFTER:
            for side in range(2):
                esend[1, side] = edges((gpl,), side)
            beside, corners, row_copies = exchange(1, (gpl,))
    arrivals = [None, send_to_core(1)]
    for b in range(3):
        for a, even0, even1, odd0, odd1 in gradients(0, b):
            turn = pltpu.roll(odd1, CH, 1)
            both = even0 + jnp.where(half, pltpu.roll(odd0, CH, 1), turn)
            start = (9 * a + 3 * b) * CH
            sums[0, start : start + 2 * CH, 0:CH] = both.T
            sums[0, start + 2 * CH : start + 3 * CH, 0:CH] = (even1 + turn).T[0:CH]
    arrivals[0] = send_to_core(0)

    merge_cores(1, arrivals[1])
    merge_cores(0, arrivals[0])
    lasts = send_to_chips()
    own_rows(gpl, 2)
    for copy in beside + corners + row_copies[0]:
        copy.wait_recv()
    finish_own(1, 0, 2)
    outer_rows(1, 0, 2)
    for hp in range(pairs):
        spread(gi_ref, hp, conv(2, hp, w3, True, range(4)).astype(BF16))

    value = window[z_here, upper, wa].astype(F32)
    for copy in lasts:
        copy.wait_recv()
    fin_ref[...] = value + jnp.sum(wgot[...].astype(F32), axis=0)
    for copy in sent:
        copy.wait_send()


def finish(sizes, gi_ref, fin_ref, gi_out, one_ref, two_ref):
    n_ha, n_wa, rows, cols = sizes
    wa = lax.axis_index("wa")
    exact = (TAPS * CH * CH) // (n_ha * n_wa)
    gi_out[...] = gi_ref[...]
    offset = lax.rem(wa * exact, 128)
    count = -(-exact // 128)
    lanes = lax.broadcasted_iota(jnp.int32, (count, 128), 1)
    for which, out in ((0, one_ref), (1, two_ref)):
        value = pltpu.roll(fin_ref[which], 128 - offset, 1)
        value = jnp.where(lanes < 128 - offset, value[0:count], value[1 : count + 1])
        for r in range(count):
            width = min(128, exact - r * 128)
            out[pl.ds(r * 128, width)] = value[r, 0:width]


def shards(sizes, inputs, grad_out, kernel_one, kernel_two):
    n_ha, n_wa, rows, cols = sizes
    rows_first = (TAPS * CH) // (2 * n_ha)
    exact = (TAPS * CH * CH) // (n_ha * n_wa)
    out_rows = -(-exact // 128)
    span = round_up(out_rows + 1, 8)
    first_pad = round_up(max(rows_first, (n_wa - 1) * rows_first // n_wa + span), 8)
    any_spec = pl.BlockSpec(memory_space=pl.ANY)
    vmem_spec = pl.BlockSpec(memory_space=pltpu.VMEM)
    dma = pltpu.SemaphoreType.DMA
    grad_inputs, fin = pl.pallas_call(
        functools.partial(kernel, sizes),
        out_shape=(
            pltpu.VMEM((rows, cols, LANES), BF16),
            pltpu.VMEM((2, span, 128), F32),
        ),
        in_specs=[pl.BlockSpec(memory_space=pltpu.HBM)] * 4,
        out_specs=(vmem_spec, vmem_spec),
        scratch_shapes=[
            pltpu.VMEM((rows, cols, LANES), BF16),
            pltpu.VMEM((rows, cols, LANES), BF16),
            pltpu.VMEM((2, TAPS, CH, CH), BF16),
            pltpu.VMEM((2, TAPS, CH, PAIR), BF16),
            pltpu.VMEM((KTOTAL, PATCH), BF16),
            pltpu.VMEM((PATCH, KTOTAL), BF16),
            pltpu.VMEM((PATCH, KTOTAL), BF16),
            pltpu.VMEM((2, 2, 16, LANES), BF16),
            pltpu.VMEM((2, 6, 16, LANES), BF16),
            pltpu.VMEM((3, 2, cols, LANES), BF16),
            pltpu.VMEM((3, 3, rows + 2, cols, PADDED), BF16),
            pltpu.VMEM((rows, cols, LANES), BF16),
            pltpu.VMEM((2, rows // 2, cols * DEPTH // 2, PATCH), F32),
            pltpu.VMEM((2, PATCH, rows * cols * 2), BF16),
            pltpu.VMEM((2, TAPS * CH, PAIR), F32),
            pltpu.VMEM((2, 2, n_ha // 2, first_pad, 128), BF16),
            pltpu.VMEM((2, n_ha // 2, first_pad, 128), BF16),
            pltpu.VMEM((n_ha // 2, first_pad, 128), F32),
            pltpu.VMEM((n_ha // 4, 2, n_wa, 2, span, 128), BF16),
            pltpu.VMEM((n_ha // 2 * n_wa - 1, 2, span, 128), BF16),
            dma((4,)),
            dma((2, 10)),
            dma((2, 10)),
            dma((2,)),
            dma((2,)),
            dma((n_ha // 2 * n_wa - 1,)),
            dma((n_ha // 2 * n_wa - 1,)),
        ],
        compiler_params=pltpu.CompilerParams(
            collective_id=0, has_side_effects=True, vmem_limit_bytes=65024 * 1024
        ),
    )(inputs, grad_out, kernel_one, kernel_two)
    return pl.pallas_call(
        functools.partial(finish, sizes),
        out_shape=(
            jax.ShapeDtypeStruct((rows, cols, LANES), BF16),
            jax.ShapeDtypeStruct((exact,), F32),
            jax.ShapeDtypeStruct((exact,), F32),
        ),
        in_specs=[vmem_spec, vmem_spec],
        out_specs=(vmem_spec, vmem_spec, vmem_spec),
        compiler_params=pltpu.CompilerParams(vmem_limit_bytes=8 * 1024 * 1024),
    )(grad_inputs, fin)


def solution(mesh):
    n_ha, n_wa = mesh.shape["ha"], mesh.shape["wa"]

    def step(inputs, grad_out, kernel_one, kernel_two):
        rows, cols, _ = inputs.shape
        return shards((n_ha, n_wa, rows, cols), inputs, grad_out, kernel_one, kernel_two)

    return jax.shard_map(
        step,
        mesh=mesh,
        in_specs=(P("ha", "wa", None), P("ha", "wa", None), P(), P()),
        out_specs=(P("ha", "wa", None), P(("ha", "wa")), P(("ha", "wa"))),
        check_vma=False,
    )
```

```python
import functools

import jax
import jax.numpy as jnp
from jax import lax
from jax.experimental import pallas as pl
from jax.experimental.pallas import tpu as pltpu
from jax.sharding import PartitionSpec as P

CH = 64
DEPTH = 8
TAPS = 27
LANES = DEPTH * CH
PADDED = LANES + 2 * CH
PAIR = 2 * CH
PATCH = 4 * CH
KTOTAL = 3 * 16 * CH
MESH = pl.DeviceIdType.MESH
SENT_AFTER = 2
F32 = jnp.float32
BF16 = jnp.bfloat16

root_half = 0.7071067811865476
inv_root_two_pi = 0.3989422804014327


def round_up(value, multiple):
    return -(-value // multiple) * multiple


def kernel(
    sizes,
    x_hbm,
    g_hbm,
    k1_hbm,
    k2_hbm,
    gi_ref,
    fin_ref,
    xl,
    gl,
    kraw,
    kd,
    w1,
    w2,
    w3,
    esend,
    erecv,
    rowbuf,
    shifted,
    gpl,
    held,
    turned,
    sums,
    piece,
    got,
    total,
    window,
    wgot,
    local_sem,
    halo_send,
    halo_recv,
    core_send,
    core_recv,
    last_send,
    last_recv,
):
    n_ha, n_wa, rows, cols = sizes
    ha = lax.axis_index("ha")
    wa = lax.axis_index("wa")
    pairs = rows // 2
    rows_first = (TAPS * CH) // (2 * n_ha)
    exact = (TAPS * CH * CH) // (n_ha * n_wa)

    def wrap(value, size):
        value = jnp.where(value >= size, value - size, value)
        return jnp.where(value < 0, value + size, value)

    def ha_at(step):
        return wrap(ha + step, n_ha)

    def wa_at(step):
        return wrap(wa + step, n_wa)

    n_z = n_ha // 4
    core = lax.rem(ha, 2)
    upper = lax.rem(lax.div(ha, 2), 2)
    z_here = lax.div(ha, 4)
    other_core = ha + 1 - 2 * core

    barrier = pltpu.get_barrier_semaphore()
    peers = [(ha_at(a), wa) for a in (-1, 1)]
    peers += [(ha, wa_at(d)) for d in (-1, 1)[: n_wa - 1]]
    peers += [(ha_at(a), wa_at(b)) for a in (-1, 1) for b in (-1, 1)]
    chips = []
    for dz in range(n_z):
        for du in range(2):
            for dw in range(n_wa):
                if dz + du + dw:
                    to_z = wrap(z_here + dz, n_z)
                    to_u = upper if du == 0 else 1 - upper
                    far = min(dz, n_z - dz) + 2 * du + min(dw, n_wa - dw)
                    peer = (to_z * 4 + to_u * 2 + core, wa_at(dw))
                    chips.append((-far, (to_z, to_u, wa_at(dw)), peer))
                    if dz + du or 1 < dw < n_wa - 1:
                        peers.append(peer)
    chips = [entry[1:] for entry in sorted(chips, key=lambda entry: entry[0])]
    loads = [
        pltpu.make_async_copy(x_hbm, xl, local_sem.at[2]),
        pltpu.make_async_copy(g_hbm, gl, local_sem.at[3]),
        pltpu.make_async_copy(k1_hbm, kraw.at[0], local_sem.at[0]),
        pltpu.make_async_copy(k2_hbm, kraw.at[1], local_sem.at[1]),
    ]
    for peer in peers[:8]:
        pl.semaphore_signal(barrier, inc=1, device_id=peer, device_id_type=MESH)
    for load in loads:
        load.start()
    for peer in peers[8:]:
        pl.semaphore_signal(barrier, inc=1, device_id=peer, device_id_type=MESH)

    sent = []

    def edges(field_refs, side):
        start, pick = (0, 0) if side == 0 else (cols - 16, 15)
        ids = lax.broadcasted_iota(jnp.int32, (2 * rows, LANES), 0)
        value = jnp.zeros((2 * rows, LANES), F32)
        for f, ref in enumerate(field_refs):
            for h in range(rows):
                block = ref[h, start : start + 16, :].astype(F32)
                cell = jnp.broadcast_to(block[pick : pick + 1], (2 * rows, LANES))
                value = jnp.where(ids == f * rows + h, cell, value)
        return value.astype(BF16)

    def exchange(phase, field_refs):
        rows_of = []
        for f, ref in enumerate(field_refs):
            slot = phase * 2 + f
            group = []
            for side, row, step in ((0, rows - 1, 1), (1, 0, -1)):
                group.append(
                    pltpu.make_async_remote_copy(
                        src_ref=ref.at[row],
                        dst_ref=rowbuf.at[slot, side],
                        send_sem=halo_send.at[phase, f * 2 + side],
                        recv_sem=halo_recv.at[phase, f * 2 + side],
                        device_id=(ha_at(step), wa),
                        device_id_type=MESH,
                    )
                )
            rows_of.append(group)
        corners = []
        for side, wa_step in ((0, -1), (1, 1)):
            for dh in (-1, 0, 1):
                slot = (1 - side) * 3 + 1 - dh
                corners.append(
                    pltpu.make_async_remote_copy(
                        src_ref=esend.at[phase, side],
                        dst_ref=erecv.at[phase, slot],
                        send_sem=halo_send.at[phase, 4 + slot],
                        recv_sem=halo_recv.at[phase, 4 + slot],
                        device_id=(ha_at(dh), wa_at(wa_step)),
                        device_id_type=MESH,
                    )
                )
        beside = [corners[1], corners[4]]
        corners = [corners[i] for i in (0, 2, 3, 5)]
        for group in [beside, rows_of[0], corners] + rows_of[1:]:
            for copy in group:
                copy.start()
            sent.extend(group)
        return beside, corners, rows_of

    def widen(value):
        zeros = jnp.zeros((value.shape[0], PADDED - LANES), F32)
        return pltpu.roll(jnp.concatenate([value, zeros], axis=1), CH, 1)

    low_ok = ha > 0
    high_ok = ha < n_ha - 1
    left_ok = wa > 0
    right_ok = wa < n_wa - 1
    cell_ids = lax.broadcasted_iota(jnp.int32, (cols, PADDED), 0)
    tile_ids = lax.broadcasted_iota(jnp.int32, (16, PADDED), 0)

    def own_rows(ref, dst):
        for h in range(rows):
            value = widen(ref[h].astype(F32))
            shifted[dst, 0, h + 1] = pltpu.roll(value, 1, 0).astype(BF16)
            shifted[dst, 1, h + 1] = value.astype(BF16)
            shifted[dst, 2, h + 1] = pltpu.roll(value, cols - 1, 0).astype(BF16)

    def halo_cells(phase, side, r):
        ok = (left_ok, right_ok)[side]
        if r != 1:
            ok = jnp.logical_and(ok, (low_ok, None, high_ok)[r])
        return jnp.where(ok, widen(erecv[phase, side * 3 + r].astype(F32)), 0.0)

    def finish_own(phase, f, dst):
        sides = [halo_cells(phase, side, 1) for side in range(2)]
        for h in range(rows):
            left = sides[0][f * rows + h : f * rows + h + 1]
            right = sides[1][f * rows + h : f * rows + h + 1]
            tile = shifted[dst, 0, h + 1, 0:16, :].astype(F32)
            tile = jnp.where(tile_ids == 0, jnp.broadcast_to(left, (16, PADDED)), tile)
            shifted[dst, 0, h + 1, 0:16, :] = tile.astype(BF16)
            tile = shifted[dst, 2, h + 1, cols - 16 : cols, :].astype(F32)
            tile = jnp.where(tile_ids == 15, jnp.broadcast_to(right, (16, PADDED)), tile)
            shifted[dst, 2, h + 1, cols - 16 : cols, :] = tile.astype(BF16)

    def outer_rows(phase, f, dst):
        slot = phase * 2 + f
        for e, side, ok, r, h in ((0, 0, low_ok, 0, rows - 1), (rows + 1, 1, high_ok, 2, 0)):
            value = widen(jnp.where(ok, rowbuf[slot, side].astype(F32), 0.0))
            left = halo_cells(phase, 0, r)[f * rows + h : f * rows + h + 1]
            right = halo_cells(phase, 1, r)[f * rows + h : f * rows + h + 1]
            before = jnp.where(
                cell_ids == 0,
                jnp.broadcast_to(left, (cols, PADDED)),
                pltpu.roll(value, 1, 0),
            )
            after = jnp.where(
                cell_ids == cols - 1,
                jnp.broadcast_to(right, (cols, PADDED)),
                pltpu.roll(value, cols - 1, 0),
            )
            shifted[dst, 0, e] = before.astype(BF16)
            shifted[dst, 1, e] = value.astype(BF16)
            shifted[dst, 2, e] = after.astype(BF16)

    lane_low = lax.broadcasted_iota(jnp.int32, (CH, PAIR), 1) < CH
    zero_block = jnp.zeros((CH, PAIR), BF16)

    def double():
        @pl.loop(0, 9)
        def _(ab):
            for c in range(3):
                for which in range(2):
                    block = kraw[which, ab * 3 + c]
                    kd[which, ab * 3 + c] = jnp.concatenate([block, block], axis=1)

    def tap_block(which, index, c):
        return kd[which, index(c)] if 0 <= c <= 2 else zero_block

    def build_rows(which, dst):
        @pl.loop(0, 3)
        def _(b):
            base = b * 16 * CH
            for di in range(4):
                for a in range(4):
                    if a < 3:
                        index = lambda c: 9 * a + 3 * b + c
                        tile = jnp.where(
                            lane_low,
                            tap_block(which, index, di),
                            tap_block(which, index, di - 1),
                        )
                    else:
                        tile = zero_block
                    here = pl.multiple_of(base + (a * 4 + di) * CH, CH)
                    dst[pl.ds(here, CH), 0:PAIR] = tile
                    here = pl.multiple_of(base + ((a + 1) % 4 * 4 + di) * CH, CH)
                    dst[pl.ds(here, CH), PAIR : 2 * PAIR] = tile

    def build_turned(which, dst):
        @pl.loop(0, 3)
        def _(b):
            base = b * 16 * CH
            for dd in range(2):
                for m in range(2):
                    for a in range(4):
                        if a < 3:
                            index = lambda c: TAPS - 1 - (9 * a + 3 * b + c)
                            tile = jnp.where(
                                lane_low,
                                tap_block(which, index, 2 * m - dd),
                                tap_block(which, index, 2 * m + 1 - dd),
                            )
                        else:
                            tile = zero_block
                        here = pl.multiple_of(base + (a * 4 + 2 * m) * CH, 128)
                        dst[dd * CH : (dd + 1) * CH, pl.ds(here, PAIR)] = tile
                        here = pl.multiple_of(base + ((a + 1) % 4 * 4 + 2 * m) * CH, 128)
                        dst[PAIR + dd * CH : PAIR + (dd + 1) * CH, pl.ds(here, PAIR)] = tile

    loads[0].wait()
    loads[1].wait()
    for side in range(2):
        esend[0, side] = edges((xl, gl), side)
    pl.semaphore_wait(barrier, len(peers))
    beside, corners, row_copies = exchange(0, (xl, gl))

    loads[2].wait()
    loads[3].wait()
    double()
    build_rows(0, w1)
    build_turned(1, w2)
    build_turned(0, w3)
    own_rows(xl, 0)
    own_rows(gl, 1)

    for copy in beside:
        copy.wait_recv()
    finish_own(0, 0, 0)
    finish_own(0, 1, 1)

    def patches(src, b, i, hp):
        return jnp.concatenate(
            [
                shifted[src, b, 2 * hp + i, :, dp * PAIR : dp * PAIR + PATCH]
                for dp in range(DEPTH // 2)
            ],
            axis=0,
        )

    def inner(hp):
        return [i for i in range(4) if 0 < 2 * hp + i < rows + 1]

    def outer(hp):
        return [i for i in range(4) if i not in inner(hp)]

    def conv(src, hp, weights, flipped, window_rows):
        spots = [(b, i) for b in range(3) for i in window_rows]
        left = jnp.concatenate([patches(src, b, i, hp) for b, i in spots], axis=1)
        parts = [slice((b * 4 + i) * PATCH, (b * 4 + i + 1) * PATCH) for b, i in spots]
        if flipped:
            right = jnp.concatenate([weights[:, part] for part in parts], axis=1)
            dims = (((1,), (1,)), ((), ()))
        else:
            right = jnp.concatenate([weights[part, :] for part in parts], axis=0)
            dims = (((1,), (0,)), ((), ()))
        return lax.dot_general(left, right, dims, preferred_element_type=F32)

    def spread(dst, hp, value):
        for hh in range(2):
            for dp in range(DEPTH // 2):
                dst[2 * hp + hh, :, dp * PAIR : (dp + 1) * PAIR] = value[
                    dp * cols : (dp + 1) * cols, hh * PAIR : (hh + 1) * PAIR
                ]

    block = cols * (DEPTH // 2)
    for hp in range(pairs):
        held[0, hp] = conv(0, hp, w1, False, inner(hp))
        held[1, hp] = conv(1, hp, w2, True, inner(hp))
    for copy in row_copies[0] + corners:
        copy.wait_recv()
    outer_rows(0, 0, 0)
    for hp in range(pairs):
        pre = held[0, hp] + conv(0, hp, w1, False, outer(hp))
        phi = 0.5 * (1.0 + lax.erf(pre * root_half))
        turned[1, :, hp * block : (hp + 1) * block] = (pre * phi).astype(BF16).T
        held[0, hp] = phi + pre * inv_root_two_pi * jnp.exp(-0.5 * pre * pre)
    for copy in row_copies[1]:
        copy.wait_recv()
    outer_rows(0, 1, 1)
    for hp in range(pairs):
        grad_active = held[1, hp] + conv(1, hp, w2, True, outer(hp))
        grad_pre = (grad_active * held[0, hp]).astype(BF16)
        spread(gpl, hp, grad_pre)
        turned[0, :, hp * block : (hp + 1) * block] = grad_pre.T

    half = lax.broadcasted_iota(jnp.int32, (CH, PAIR), 1) < CH

    def gradients(src, b):
        blocks = []
        for i in range(4):
            right = jnp.concatenate([patches(src, b, i, hp) for hp in range(pairs)], axis=0)
            blocks.append(
                lax.dot_general(
                    turned[src],
                    right,
                    (((1,), (0,)), ((), ())),
                    preferred_element_type=F32,
                )
            )
        for a in range(3):
            low, high = blocks[a], blocks[a + 1]
            even = low[0:CH] + high[PAIR : PAIR + CH]
            odd = low[CH:PAIR] + high[PAIR + CH : 2 * PAIR]
            yield a, even[:, :PAIR], even[:, PAIR:], odd[:, :PAIR], odd[:, PAIR:]

    def send_to_core(which):
        for j in range(n_ha):
            first = sums[which, pl.ds(2 * j * rows_first, rows_first, stride=2), :]
            second = sums[which, pl.ds(2 * j * rows_first + 1, rows_first, stride=2), :]
            value = jnp.where(
                lax.broadcasted_iota(jnp.int32, (rows_first, PAIR), 1) < CH,
                first,
                pltpu.roll(second, CH, 1),
            )
            piece[which, j % 2, j // 2, 0:rows_first, :] = value.astype(BF16)
        copy = pltpu.make_async_remote_copy(
            src_ref=piece.at[which, 1 - core],
            dst_ref=got.at[which],
            send_sem=core_send.at[which],
            recv_sem=core_recv.at[which],
            device_id=(other_core, wa),
            device_id_type=MESH,
        )
        copy.start()
        sent.append(copy)
        return copy

    starts = [(k * rows_first) // n_wa for k in range(n_wa)]
    span = window.shape[4]

    def merge_cores(which, arrival):
        arrival.wait_recv()
        for t in range(n_ha // 2):
            total[t] = piece[which, core, t].astype(F32) + got[which, t].astype(F32)
        for t in range(n_ha // 2):
            for k in range(n_wa):
                value = total[t, starts[k] : starts[k] + span, :]
                window[t // 2, t % 2, k, which] = value.astype(BF16)

    def send_to_chips():
        copies = []
        for i, ((to_z, to_u, to_w), peer) in enumerate(chips):
            copies.append(
                pltpu.make_async_remote_copy(
                    src_ref=window.at[to_z, to_u, to_w],
                    dst_ref=wgot.at[i],
                    send_sem=last_send.at[i],
                    recv_sem=last_recv.at[i],
                    device_id=peer,
                    device_id_type=MESH,
                )
            )
        for copy in copies:
            copy.start()
        sent.extend(copies)
        return copies

    for b in range(3):
        for a, even0, even1, odd0, odd1 in gradients(1, b):
            turn = pltpu.roll(odd1, CH, 1)
            values = (even0 + pltpu.roll(odd0, CH, 1), odd1 + pltpu.roll(even0, CH, 1), even1 + turn)
            for c in range(3):
                start = (TAPS - 1 - (9 * a + 3 * b + c)) * CH
                sums[1, start : start + CH, :] = values[c]
        if b == SENT_AFTER:
            for side in range(2):
                esend[1, side] = edges((gpl,), side)
            beside, corners, row_copies = exchange(1, (gpl,))
    arrivals = [None, send_to_core(1)]
    for b in range(3):
        for a, even0, even1, odd0, odd1 in gradients(0, b):
            turn = pltpu.roll(odd1, CH, 1)
            both = even0 + jnp.where(half, pltpu.roll(odd0, CH, 1), turn)
            start = (9 * a + 3 * b) * CH
            sums[0, start : start + 2 * CH, 0:CH] = both.T
            sums[0, start + 2 * CH : start + 3 * CH, 0:CH] = (even1 + turn).T[0:CH]
    arrivals[0] = send_to_core(0)

    merge_cores(1, arrivals[1])
    merge_cores(0, arrivals[0])
    lasts = send_to_chips()
    own_rows(gpl, 2)
    for copy in beside + corners + row_copies[0]:
        copy.wait_recv()
    finish_own(1, 0, 2)
    outer_rows(1, 0, 2)
    for hp in range(pairs):
        spread(gi_ref, hp, conv(2, hp, w3, True, range(4)).astype(BF16))

    value = window[z_here, upper, wa].astype(F32)
    for copy in sent:
        copy.wait_send()
    for copy in lasts:
        copy.wait_recv()
    fin_ref[...] = value + jnp.sum(wgot[...].astype(F32), axis=0)


def finish(sizes, gi_ref, fin_ref, gi_out, one_ref, two_ref):
    n_ha, n_wa, rows, cols = sizes
    wa = lax.axis_index("wa")
    exact = (TAPS * CH * CH) // (n_ha * n_wa)
    gi_out[...] = gi_ref[...]
    offset = lax.rem(wa * exact, 128)
    count = -(-exact // 128)
    lanes = lax.broadcasted_iota(jnp.int32, (count, 128), 1)
    for which, out in ((0, one_ref), (1, two_ref)):
        value = pltpu.roll(fin_ref[which], 128 - offset, 1)
        value = jnp.where(lanes < 128 - offset, value[0:count], value[1 : count + 1])
        for r in range(count):
            width = min(128, exact - r * 128)
            out[pl.ds(r * 128, width)] = value[r, 0:width]


def shards(sizes, inputs, grad_out, kernel_one, kernel_two):
    n_ha, n_wa, rows, cols = sizes
    rows_first = (TAPS * CH) // (2 * n_ha)
    exact = (TAPS * CH * CH) // (n_ha * n_wa)
    out_rows = -(-exact // 128)
    span = round_up(out_rows + 1, 8)
    first_pad = round_up(max(rows_first, (n_wa - 1) * rows_first // n_wa + span), 8)
    any_spec = pl.BlockSpec(memory_space=pl.ANY)
    vmem_spec = pl.BlockSpec(memory_space=pltpu.VMEM)
    dma = pltpu.SemaphoreType.DMA
    grad_inputs, fin = pl.pallas_call(
        functools.partial(kernel, sizes),
        out_shape=(
            pltpu.VMEM((rows, cols, LANES), BF16),
            pltpu.VMEM((2, span, 128), F32),
        ),
        in_specs=[pl.BlockSpec(memory_space=pltpu.HBM)] * 4,
        out_specs=(vmem_spec, vmem_spec),
        scratch_shapes=[
            pltpu.VMEM((rows, cols, LANES), BF16),
            pltpu.VMEM((rows, cols, LANES), BF16),
            pltpu.VMEM((2, TAPS, CH, CH), BF16),
            pltpu.VMEM((2, TAPS, CH, PAIR), BF16),
            pltpu.VMEM((KTOTAL, PATCH), BF16),
            pltpu.VMEM((PATCH, KTOTAL), BF16),
            pltpu.VMEM((PATCH, KTOTAL), BF16),
            pltpu.VMEM((2, 2, 2 * rows, LANES), BF16),
            pltpu.VMEM((2, 6, 2 * rows, LANES), BF16),
            pltpu.VMEM((3, 2, cols, LANES), BF16),
            pltpu.VMEM((3, 3, rows + 2, cols, PADDED), BF16),
            pltpu.VMEM((rows, cols, LANES), BF16),
            pltpu.VMEM((2, rows // 2, cols * DEPTH // 2, PATCH), F32),
            pltpu.VMEM((2, PATCH, rows * cols * 2), BF16),
            pltpu.VMEM((2, TAPS * CH, PAIR), F32),
            pltpu.VMEM((2, 2, n_ha // 2, first_pad, 128), BF16),
            pltpu.VMEM((2, n_ha // 2, first_pad, 128), BF16),
            pltpu.VMEM((n_ha // 2, first_pad, 128), F32),
            pltpu.VMEM((n_ha // 4, 2, n_wa, 2, span, 128), BF16),
            pltpu.VMEM((n_ha // 2 * n_wa - 1, 2, span, 128), BF16),
            dma((4,)),
            dma((2, 10)),
            dma((2, 10)),
            dma((2,)),
            dma((2,)),
            dma((n_ha // 2 * n_wa - 1,)),
            dma((n_ha // 2 * n_wa - 1,)),
        ],
        compiler_params=pltpu.CompilerParams(
            collective_id=0, has_side_effects=True, vmem_limit_bytes=65024 * 1024
        ),
    )(inputs, grad_out, kernel_one, kernel_two)
    return pl.pallas_call(
        functools.partial(finish, sizes),
        out_shape=(
            jax.ShapeDtypeStruct((rows, cols, LANES), BF16),
            jax.ShapeDtypeStruct((exact,), F32),
            jax.ShapeDtypeStruct((exact,), F32),
        ),
        in_specs=[vmem_spec, vmem_spec],
        out_specs=(vmem_spec, vmem_spec, vmem_spec),
        compiler_params=pltpu.CompilerParams(vmem_limit_bytes=8 * 1024 * 1024),
    )(grad_inputs, fin)


def solution(mesh):
    n_ha, n_wa = mesh.shape["ha"], mesh.shape["wa"]

    def step(inputs, grad_out, kernel_one, kernel_two):
        rows, cols, _ = inputs.shape
        return shards((n_ha, n_wa, rows, cols), inputs, grad_out, kernel_one, kernel_two)

    return jax.shard_map(
        step,
        mesh=mesh,
        in_specs=(P("ha", "wa", None), P("ha", "wa", None), P(), P()),
        out_specs=(P("ha", "wa", None), P(("ha", "wa")), P(("ha", "wa"))),
        check_vma=False,
    )
```
